128 devices in a mesh: narrow: 8 (over y, core), wide: 16 (over x, z).
Axes of the slice: x: 4, y: 4, z: 4, core: 2. Of those that a mesh axis runs over, the one named last changes fastest.
Arguments:
- rhs_field: float32 [2, 131072, 768], P(None, ('wide', 'narrow')), may hold values from -6 to 6
- leaf_inverse: float32 [2, 131072, 512], P(None, ('wide', 'narrow')), may hold values from -0.1875 to 0.1875
- expand_one: float32 [2, 131072, 128], P(None, ('wide', 'narrow')), may hold values from -0.375 to 0.375
- project_one: float32 [2, 131072, 128], P(None, ('wide', 'narrow')), may hold values from -0.046875 to 0.046875
- core_one: float32 [2, 2048, 256], P(None, 'wide'), may hold values from -0.25 to 0.25
- expand_two: float32 [2, 131072, 128], P(None, ('wide', 'narrow')), may hold values from -0.375 to 0.375
- project_two: float32 [2, 131072, 128], P(None, ('wide', 'narrow')), may hold values from -0.0234375 to 0.0234375
- core_two: float32 [2, 512, 256], replicated, may hold values from -0.25 to 0.25
- expand_three: float32 [2, 131072, 128], P(None, ('wide', 'narrow')), may hold values from -0.375 to 0.375
- project_three: float32 [2, 131072, 128], P(None, ('wide', 'narrow')), may hold values from -0.015625 to 0.015625
- core_three: float32 [2, 256, 256], replicated, may hold values from -0.25 to 0.25
Outputs:
- solution: float32 [2, 131072, 768], P(None, ('wide', 'narrow'))
The draws below stay inside these ranges and needn't reach their ends.
All inputs are finite; a program needn't handle non-finite values.
Results may differ from the reference program's by a relative error of at most 0.0003.
Values sent between devices are 32-bit elements; how exact they have to be, the bound alone decides.
A program may use at most 128 MiB of HBM per device.

```python
import jax
import jax.numpy as jnp
from jax import lax

LEAF = 512
RANK = 128
NRHS = 768
ROWS_DEV = 1024
N = 131072
KIDS_ONE = 16
N_NARROW = 8
N_WIDE = 16


def steps_of(rng, extent, shards, low, top_value):
    def one(dim, shards_of):
        draws = jax.random.uniform(jax.random.fold_in(jax.random.fold_in(rng, 6), dim), (shards_of,), jnp.float32, low / len(shards), top_value / len(shards))
        return jnp.repeat(jnp.exp(draws), extent[dim] // shards_of).reshape((-1,) + (1,) * (len(extent) - dim - 1))

    gain = one(*shards[0])
    for cut in shards[1:]:
        gain = gain * one(*cut)
    return gain


def normal_values(key, dims, scale, bound, split=(), dtype=jnp.bfloat16):
    entries = jax.random.normal(key, dims, jnp.float32) * scale
    if len(split) > 0:
        entries = steps_of(key, dims, split, -0.22, 0.18) * entries
    return jnp.clip(entries, min=-bound, max=bound).astype(dtype)


def setup_inputs(seed: int = 0) -> dict:
    arg_keys = jax.random.split(jax.random.key(seed), 12)
    rhs_field = normal_values(arg_keys[0], (2, N, NRHS), 1.0, 6.0, ((1, 128),), jnp.float32)
    leaf_inverse = normal_values(arg_keys[1], (2, N, LEAF), (2 * LEAF) ** -0.5, 0.1875, ((1, 128),), jnp.float32)
    expand_one = normal_values(arg_keys[2], (2, N, RANK), (2 * RANK) ** -0.5, 0.375, ((1, 128),), jnp.float32)
    project_one = normal_values(arg_keys[3], (2, N, RANK), (2 * N_NARROW * ROWS_DEV) ** -0.5, 0.046875, ((1, 128),), jnp.float32)
    core_one = normal_values(arg_keys[4], (2, KIDS_ONE * RANK, 2 * RANK), (4 * RANK) ** -0.5, 0.25, ((1, 16),), jnp.float32)
    expand_two = normal_values(arg_keys[5], (2, N, RANK), (2 * RANK) ** -0.5, 0.375, ((1, 128),), jnp.float32)
    project_two = normal_values(arg_keys[6], (2, N, RANK), (N // 2) ** -0.5, 0.0234375, ((1, 128),), jnp.float32)
    core_two = normal_values(arg_keys[7], (2, 4 * RANK, 2 * RANK), (4 * RANK) ** -0.5, 0.25, (), jnp.float32)
    expand_three = normal_values(arg_keys[8], (2, N, RANK), (2 * RANK) ** -0.5, 0.375, ((1, 128),), jnp.float32)
    project_three = normal_values(arg_keys[9], (2, N, RANK), N ** -0.5, 0.015625, ((1, 128),), jnp.float32)
    core_three = normal_values(arg_keys[10], (2, 2 * RANK, 2 * RANK), (4 * RANK) ** -0.5, 0.25, (), jnp.float32)
    return {"rhs_field": rhs_field, "leaf_inverse": leaf_inverse, "expand_one": expand_one, "project_one": project_one, "core_one": core_one, "expand_two": expand_two, "project_two": project_two, "core_two": core_two, "expand_three": expand_three, "project_three": project_three, "core_three": core_three}


def complex_product(form, first_factor, second_factor):
    highest = lax.Precision.HIGHEST
    plain = jnp.einsum(form, first_factor[0], second_factor[0], precision=highest)
    crossed = jnp.einsum(form, first_factor[1], second_factor[1], precision=highest)
    summed = jnp.einsum(form, first_factor[0] + first_factor[1], second_factor[0] + second_factor[1], precision=highest)
    return plain - crossed, summed - plain - crossed


def reference(rhs_field, leaf_inverse, expand_one, project_one, core_one, expand_two, project_two, core_two, expand_three, project_three, core_three):
    row_count = rhs_field.shape[1]
    columns = rhs_field.shape[2]
    leaves = row_count // LEAF
    inverse = leaf_inverse.reshape(2, leaves, LEAF, LEAF)
    source = rhs_field.reshape(2, leaves, LEAF, columns)
    solved = complex_product("lij,ljn->lin", (inverse[0], inverse[1]), (source[0], source[1]))
    current = (solved[0].reshape(row_count, columns), solved[1].reshape(row_count, columns))
    levels = ((expand_one, project_one, core_one, N_WIDE), (expand_two, project_two, core_two, 4), (expand_three, project_three, core_three, 2))
    for expand, project, core, children in levels:
        child_rows = row_count // children
        bases = (project[0].reshape(children, child_rows, RANK), -project[1].reshape(children, child_rows, RANK))
        pieces = (current[0].reshape(children, child_rows, columns), current[1].reshape(children, child_rows, columns))
        projected = complex_product("csr,csn->crn", bases, pieces)
        stacked = (projected[0].reshape(children // 2, 2 * RANK, columns), projected[1].reshape(children // 2, 2 * RANK, columns))
        core_blocks = (core[0].reshape(children // 2, 2 * RANK, 2 * RANK), core[1].reshape(children // 2, 2 * RANK, 2 * RANK))
        correction = complex_product("bij,bjn->bin", core_blocks, stacked)
        correction = (correction[0].reshape(children, RANK, columns), correction[1].reshape(children, RANK, columns))
        expanders = (expand[0].reshape(children, child_rows, RANK), expand[1].reshape(children, child_rows, RANK))
        update = complex_product("csr,crn->csn", expanders, correction)
        current = (current[0] - update[0].reshape(row_count, columns), current[1] - update[1].reshape(row_count, columns))
    return jnp.stack(current)
```

```python
import functools

import jax
import jax.numpy as jnp
from jax import lax
from jax.experimental import pallas as pl
from jax.experimental.pallas import tpu as pltpu
from jax.sharding import PartitionSpec as P

MESH = pl.DeviceIdType.MESH
F32 = jnp.float32
BF16 = jnp.bfloat16
LEAF = 512
R = 128
NR = 768
ROWS = 1024
SL = 96
SUB = 24
NT = (((1,), (1,)), ((), ()))


def halves(x):
    hi = x.astype(BF16)
    return hi, (x - hi.astype(F32)).astype(BF16)


def dot_nn(a_hi, a_lo, b_hi, b_lo):
    a = jnp.concatenate([a_hi, a_lo, a_hi], axis=1)
    b = jnp.concatenate([b_hi, b_hi, b_lo], axis=0)
    return jnp.dot(a, b, preferred_element_type=F32)


def combine(t):
    return t[0] - t[1], t[2] - t[0] - t[1]


def small_product(re, im, cat_ref):
    t = []
    for v, x in enumerate((re, im, re + im)):
        hi, lo = halves(x)
        t.append(
            lax.dot_general(
                jnp.concatenate([hi, lo, hi], axis=1),
                cat_ref[v],
                NT,
                preferred_element_type=F32,
            )
        )
    return combine(t)


def store_cat(cat_ref, re, im):
    for v, x in enumerate((re, im, re + im)):
        hi, lo = halves(x)
        cat_ref[v] = jnp.concatenate([hi, hi, lo], axis=1)


def main_kernel(
    rhs, leaf, e1, p1, c1, e2, p2, c2, p3, c3,
    y0_out, corr_out,
    rhs_v, leaf_v, e_v, p_v, c1_v, c2_v, c3_v,
    lhi, llo, yhi, ylo, pthi, ptlo,
    zt, pair_buf, rs_buf, corr, g_loc, g_rs, g_full, gcat,
    c1cat, c2cat, c3cat, stk1, t2, rz2, stk2, t3, rz3, v3,
    in_sem, send_sem, recv_sem,
):
    n = lax.axis_index("narrow")
    w = lax.axis_index("wide")
    y, c = n // 2, lax.rem(n, 2)
    x, z = w // 4, lax.rem(w, 4)
    partner = n + 1 - 2 * c

    def dev(nn, ww):
        return {"narrow": nn, "wide": ww}

    def y_at(d):
        return lax.rem(y + d, 4)

    def z_at(d):
        return x * 4 + lax.rem(z + d, 4)

    def x_at(d):
        return lax.rem(x + d, 4) * 4 + z

    def rows_of(slot):
        return pl.ds(pl.multiple_of(slot * SL, 8), SL)

    sends = []

    def send(src, dst, idx, device):
        copy = pltpu.make_async_remote_copy(
            src_ref=src, dst_ref=dst, send_sem=send_sem.at[idx], recv_sem=recv_sem.at[idx],
            device_id=device, device_id_type=MESH,
        )
        copy.start()
        sends.append(copy)
        return copy

    pending = {}

    def fetch(name, src, dst, idx):
        copy = pltpu.make_async_copy(src, dst, in_sem.at[idx])
        copy.start()
        pending[name] = copy

    fetch("p2", p2, p_v.at[1], 0)
    fetch("p3", p3, p_v.at[2], 1)
    fetch("e1", e1, e_v.at[0], 2)
    fetch("e2", e2, e_v.at[1], 3)
    fetch("p1", p1, p_v.at[0], 4)
    for l in range(2):
        rows = pl.ds(l * LEAF, LEAF)
        fetch("leaf%d" % l, leaf.at[:, rows, :], leaf_v.at[:, rows, :], 5 + 2 * l)
        fetch("rhs%d" % l, rhs.at[:, rows, :], rhs_v.at[:, rows, :], 6 + 2 * l)
    fetch("c1", c1, c1_v, 9)
    fetch("c2", c2.at[:, pl.ds(pl.multiple_of(x * R, R), R), :], c2_v, 10)
    fetch("c3", c3.at[:, pl.ds(pl.multiple_of((x // 2) * R, R), R), :], c3_v, 11)

    barrier = pltpu.get_barrier_semaphore()
    peers = [dev(lax.rem(n + d, 8), w) for d in range(1, 8)]
    peers += [dev(n, z_at(d)) for d in range(1, 4)] + [dev(n, x_at(d)) for d in range(1, 4)]
    for peer in peers:
        pl.semaphore_signal(barrier, inc=1, device_id=peer, device_id_type=MESH)
    pl.semaphore_wait(barrier, len(peers))

    for name in ("p2", "p3", "p1"):
        pending[name].wait()

    def prepare_projection(l, carry):
        at = pl.ds(pl.multiple_of(l * R, R), R)
        re, im = p_v[l, 0].T, p_v[l, 1].T
        for v, value in enumerate((re, -im, re - im)):
            pthi[v, at, :], ptlo[v, at, :] = halves(value)
        return carry

    lax.fori_loop(0, 3, prepare_projection, 0)

    pending["e1"].wait()
    pending["e2"].wait()
    for e, low, mats in ((0, 1, (0, 1)), (1, 2, (2,))):
        lines = pl.ds(low * R, (3 - low) * R)
        t = []
        for v, value in enumerate((e_v[e, 0], e_v[e, 1], e_v[e, 0] + e_v[e, 1])):
            hi, lo = halves(value)
            t.append(dot_nn(pthi[v, lines, :], ptlo[v, lines, :], hi, lo))
        pieces = combine(t)
        for k, m in enumerate(mats):
            for part in range(2):
                for slot in range(8):
                    g_loc[slot, 2 * m + part] = pieces[part][k * R + slot * 16 : k * R + slot * 16 + 16, :]
    g_sends = []
    for d in range(1, 8):
        to = lax.rem(n + d, 8)
        g_sends.append(send(g_loc.at[to], g_rs.at[d - 1], 13 + d - 1, dev(to, w)))

    def solve_leaf(l):
        pending["leaf%d" % l].wait()
        pending["rhs%d" % l].wait()
        rows = pl.ds(l * LEAF, LEAF)

        def split_leaf(q, carry):
            src = pl.ds(pl.multiple_of(l * LEAF + q * 128, 128), 128)
            dst = pl.ds(pl.multiple_of(q * 128, 128), 128)
            re, im = leaf_v[0, src, :], leaf_v[1, src, :]
            for v, value in enumerate((re, im, re + im)):
                lhi[v, dst, :], llo[v, dst, :] = halves(value)
            return carry

        lax.fori_loop(0, 4, split_leaf, 0)

        def tile(j, carry):
            cols = pl.ds(pl.multiple_of(j * 256, 256), 256)
            b_re, b_im = rhs_v[0, rows, cols], rhs_v[1, rows, cols]
            t = []
            for v, value in enumerate((b_re, b_im, b_re + b_im)):
                hi, lo = halves(value)
                t.append(dot_nn(lhi[v], llo[v], hi, lo))
            re, im = combine(t)
            rhs_v[0, rows, cols] = re
            rhs_v[1, rows, cols] = im
            for v, value in enumerate((re, im, re + im)):
                yhi[v, rows, cols], ylo[v, rows, cols] = halves(value)
            return carry

        lax.fori_loop(0, 3, tile, 0)
        copy = pltpu.make_async_copy(rhs_v.at[:, rows, :], y0_out.at[:, rows, :], in_sem.at[12 + l])
        copy.start()
        return copy

    outs = [solve_leaf(0)]
    for copy in g_sends:
        copy.wait_recv()
    total = g_loc[n]
    for d in range(7):
        total = total + g_rs[d]
    g_full[n] = total
    ag = []
    for d in range(1, 8):
        to = lax.rem(n + d, 8)
        ag.append(send(g_full.at[n], g_full.at[n], 20 + d - 1, dev(to, w)))
    outs.append(solve_leaf(1))

    def project(j, carry):
        cols = pl.ds(pl.multiple_of(j * 256, 256), 256)
        t = [dot_nn(pthi[v], ptlo[v], yhi[v, :, cols], ylo[v, :, cols]) for v in range(3)]
        for part, value in enumerate(combine(t)):
            for l in range(3):
                zt[l, part, cols, :] = value[l * R : (l + 1) * R, :].T
        return carry

    lax.fori_loop(0, 3, project, 0)

    pair = []
    for q in range(4):
        pair.append(send(zt.at[:, :, rows_of(2 * q + 1 - c), :], pair_buf.at[q], q, dev(partner, w)))

    for name in ("c1", "c2", "c3"):
        pending[name].wait()
    store_cat(c1cat, c1_v[0], c1_v[1])
    store_cat(c2cat, c2_v[0], c2_v[1])
    store_cat(c3cat, c3_v[0], c3_v[1])

    for q in range(4):
        pair[q].wait_recv()
        mine = rows_of(2 * q + c)
        zt[:, :, mine, :] = zt[:, :, mine, :] + pair_buf[q]
    ring = {}
    for l in range(3):
        for d in (2, 1, 3):
            ring[l, d] = send(
                zt.at[l, :, rows_of(2 * y_at(d) + c), :], rs_buf.at[l, d - 1], 4 + 3 * l + d - 1, dev(2 * y_at(d) + c, w)
            )
    for copy in ag:
        copy.wait_recv()
    for m in range(3):
        store_cat(gcat.at[m], g_full[:, 2 * m].reshape(R, R), g_full[:, 2 * m + 1].reshape(R, R))
    own = rows_of(n)

    def summed(l):
        for d in range(1, 4):
            ring[l, d].wait_recv()
        return [zt[l, part, own, :] + rs_buf[l, 0, part] + rs_buf[l, 1, part] + rs_buf[l, 2, part] for part in range(2)]

    def spread(l):
        for d in (2, 1, 3):
            ring["s", l, d] = send(corr.at[l, :, own, :], corr.at[l, :, own, :], 44 + 3 * l + d - 1, dev(2 * y_at(d) + c, w))
        ring["p", l] = send(corr.at[l, :, own, :], corr.at[l, :, own, :], 53 + l, dev(partner, w))

    def forward(l):
        for d in (1, 3, 2):
            ring["s", l, d].wait_recv()
            rows = rows_of(2 * y_at(4 - d) + c)
            ring["f", l, d] = send(corr.at[l, :, rows, :], corr.at[l, :, rows, :], 56 + 3 * l + d - 1, dev(partner, w))

    def arrive(l):
        ring["p", l].wait_recv()
        for d in (1, 3, 2):
            ring["f", l, d].wait_recv()

    b = lax.rem(z, 2)
    s1 = summed(0)
    for part in range(2):
        stk1[b, part] = s1[part]
    sib = send(stk1.at[b], stk1.at[b], 27, dev(n, w + 1 - 2 * b))
    sib.wait_recv()
    pairs = [jnp.concatenate([stk1[0, part], stk1[1, part]], axis=1) for part in range(2)]
    k1 = small_product(pairs[0], pairs[1], c1cat)
    for part in range(2):
        corr[0, part, own, :] = k1[part]
    spread(0)

    def sub_rows(q):
        return pl.ds(pl.multiple_of(n * SL + q * SUB, 8), SUB)

    g1 = small_product(k1[0], k1[1], gcat.at[0])
    s2 = summed(1)
    for part in range(2):
        value = s2[part] - g1[part]
        for q in range(4):
            t2[q, part] = value[q * SUB : (q + 1) * SUB]
    got = []
    for d in range(1, 4):
        got.append(send(t2.at[lax.rem(z + d, 4)], rz2.at[d - 1], 28 + d - 1, dev(n, z_at(d))))
    g1 = small_product(k1[0], k1[1], gcat.at[1])
    for copy in got:
        copy.wait_recv()
    xb = lax.rem(x, 2)
    stk2[xb] = t2[z] + rz2[0] + rz2[1] + rz2[2]
    copy = send(stk2.at[xb], stk2.at[xb], 31, dev(n, w + 4 - 8 * xb))
    forward(0)
    copy.wait_recv()
    pairs = [jnp.concatenate([stk2[0, part], stk2[1, part]], axis=1) for part in range(2)]
    k2 = small_product(pairs[0], pairs[1], c2cat)
    for part in range(2):
        corr[1, part, sub_rows(z), :] = k2[part]
    got = []
    for d in range(1, 4):
        got.append(send(corr.at[1, :, sub_rows(z), :], corr.at[1, :, sub_rows(z), :], 32 + d - 1, dev(n, z_at(d))))
    s3 = summed(2)
    for copy in got:
        copy.wait_recv()
    spread(1)

    g2 = small_product(corr[1, 0, own, :], corr[1, 1, own, :], gcat.at[2])
    for part in range(2):
        value = s3[part] - g1[part] - g2[part]
        for q in range(4):
            t3[q, part] = value[q * SUB : (q + 1) * SUB]
    got = []
    for d in range(1, 4):
        got.append(send(t3.at[lax.rem(z + d, 4)], rz3.at[d - 1], 35 + d - 1, dev(n, z_at(d))))
    for copy in got:
        copy.wait_recv()
    v3[x] = t3[z] + rz3[0] + rz3[1] + rz3[2]
    got = []
    for d in range(1, 4):
        got.append(send(v3.at[x], v3.at[x], 38 + d - 1, dev(n, x_at(d))))
    arrive(0)
    forward(1)
    for copy in got:
        copy.wait_recv()
    pairs = [
        jnp.concatenate([v3[0, part] + v3[1, part], v3[2, part] + v3[3, part]], axis=1) for part in range(2)
    ]
    k3 = small_product(pairs[0], pairs[1], c3cat)
    for part in range(2):
        corr[2, part, sub_rows(z), :] = k3[part]
    got = []
    for d in range(1, 4):
        got.append(send(corr.at[2, :, sub_rows(z), :], corr.at[2, :, sub_rows(z), :], 41 + d - 1, dev(n, z_at(d))))
    arrive(1)
    for copy in got:
        copy.wait_recv()
    spread(2)
    done = []
    for l in range(2):
        copy = pltpu.make_async_copy(corr.at[l], corr_out.at[l], in_sem.at[14 + l])
        copy.start()
        done.append(copy)
    forward(2)
    arrive(2)
    copy = pltpu.make_async_copy(corr.at[2], corr_out.at[2], in_sem.at[16])
    copy.start()
    done.append(copy)

    for copy in sends:
        copy.wait_send()
    for copy in outs + done:
        copy.wait()


def main_call(rhs, leaf, e1, p1, c1, e2, p2, c2, p3, c3):
    any_spec = pl.BlockSpec(memory_space=pl.ANY)
    vm = pltpu.VMEM
    return pl.pallas_call(
        main_kernel,
        out_shape=(
            jax.ShapeDtypeStruct((2, ROWS, NR), F32),
            jax.ShapeDtypeStruct((3, 2, NR, R), F32),
        ),
        in_specs=[any_spec] * 10,
        out_specs=(any_spec, any_spec),
        scratch_shapes=[
            vm((2, ROWS, NR), F32),
            vm((2, ROWS, LEAF), F32),
            vm((2, 2, ROWS, R), F32),
            vm((3, 2, ROWS, R), F32),
            vm((2, R, 2 * R), F32),
            vm((2, R, 2 * R), F32),
            vm((2, R, 2 * R), F32),
            vm((3, LEAF, LEAF), BF16),
            vm((3, LEAF, LEAF), BF16),
            vm((3, ROWS, NR), BF16),
            vm((3, ROWS, NR), BF16),
            vm((3, 3 * R, ROWS), BF16),
            vm((3, 3 * R, ROWS), BF16),
            vm((3, 2, NR, R), F32),
            vm((4, 3, 2, SL, R), F32),
            vm((3, 3, 2, SL, R), F32),
            vm((3, 2, NR, R), F32),
            vm((8, 6, 16, R), F32),
            vm((7, 6, 16, R), F32),
            vm((8, 6, 16, R), F32),
            vm((3, 3, R, 3 * R), BF16),
            vm((3, R, 6 * R), BF16),
            vm((3, R, 6 * R), BF16),
            vm((3, R, 6 * R), BF16),
            vm((2, 2, SL, R), F32),
            vm((4, 2, SUB, R), F32),
            vm((3, 2, SUB, R), F32),
            vm((2, 2, SUB, R), F32),
            vm((4, 2, SUB, R), F32),
            vm((3, 2, SUB, R), F32),
            vm((4, 2, SUB, R), F32),
            pltpu.SemaphoreType.DMA((17,)),
            pltpu.SemaphoreType.DMA((65,)),
            pltpu.SemaphoreType.DMA((65,)),
        ],
        compiler_params=pltpu.CompilerParams(
            collective_id=0, has_side_effects=True, vmem_limit_bytes=60 * 1024 * 1024
        ),
        cost_estimate=pl.CostEstimate(flops=14_000_000_000, bytes_accessed=26_000_000, transcendentals=0),
    )(rhs, leaf, e1, p1, c1, e2, p2, c2, p3, c3)


def expand_kernel(y0, e1, e2, e3, corr, out, chi, clo):
    @pl.when(pl.program_id(0) == 0)
    def _():
        for l in range(3):
            lanes = slice(l * R, (l + 1) * R)
            re, im = corr[l, 0], corr[l, 1]
            for v, value in enumerate((re, im, re + im)):
                chi[v, :, lanes], clo[v, :, lanes] = halves(value)

    e_re = jnp.concatenate([e1[0], e2[0], e3[0]], axis=1)
    e_im = jnp.concatenate([e1[1], e2[1], e3[1]], axis=1)
    t = []
    for v, value in enumerate((e_re, e_im, e_re + e_im)):
        hi, lo = halves(value)
        t.append(
            lax.dot_general(
                jnp.concatenate([hi, lo, hi], axis=1),
                jnp.concatenate([chi[v], chi[v], clo[v]], axis=1),
                NT,
                preferred_element_type=F32,
            )
        )
    re, im = combine(t)
    out[0] = y0[0] - re
    out[1] = y0[1] - im


def expand_call(y0, e1, e2, e3, corr):
    tm = 256
    rows = pl.BlockSpec((2, tm, NR), lambda i: (0, i, 0))
    base = pl.BlockSpec((2, tm, R), lambda i: (0, i, 0))
    return pl.pallas_call(
        expand_kernel,
        out_shape=jax.ShapeDtypeStruct((2, ROWS, NR), F32),
        grid=(ROWS // tm,),
        in_specs=[rows, base, base, base, pl.BlockSpec((3, 2, NR, R), lambda i: (0, 0, 0, 0))],
        out_specs=rows,
        scratch_shapes=[pltpu.VMEM((3, NR, 3 * R), BF16), pltpu.VMEM((3, NR, 3 * R), BF16)],
        compiler_params=pltpu.CompilerParams(
            dimension_semantics=("arbitrary",), vmem_limit_bytes=48 * 1024 * 1024
        ),
        cost_estimate=pl.CostEstimate(flops=5_400_000_000, bytes_accessed=18_000_000, transcendentals=0),
    )(y0, e1, e2, e3, corr)


def body(rhs, leaf, e1, p1, c1, e2, p2, c2, e3, p3, c3):
    y0, corr = main_call(rhs, leaf, e1, p1, c1, e2, p2, c2, p3, c3)
    return expand_call(y0, e1, e2, e3, corr)


def solution(mesh):
    split = P(None, ("wide", "narrow"), None)
    placed = (split, split, split, split, P(None, "wide", None), split, split, P(), split, split, P())
    return jax.shard_map(body, mesh=mesh, in_specs=placed, out_specs=split, check_vma=False)
```

```python
import functools

import jax
import jax.numpy as jnp
from jax import lax
from jax.experimental import pallas as pl
from jax.experimental.pallas import tpu as pltpu
from jax.sharding import PartitionSpec as P

MESH = pl.DeviceIdType.MESH
F32 = jnp.float32
BF16 = jnp.bfloat16
LEAF = 512
R = 128
NR = 768
ROWS = 1024
TILE = 256
NSEM = 120
NT = (((1,), (1,)), ((), ()))


def halves(x):
    hi = x.astype(BF16)
    return hi, (x - hi.astype(F32)).astype(BF16)


def dot_nn(a_hi, a_lo, b_hi, b_lo):
    a = jnp.concatenate([a_hi, a_lo, a_hi], axis=1)
    b = jnp.concatenate([b_hi, b_hi, b_lo], axis=0)
    return jnp.dot(a, b, preferred_element_type=F32)


def combine(t):
    return t[0] - t[1], t[2] - t[0] - t[1]


def small_product(re, im, cat_ref):
    t = []
    for v, x in enumerate((re, im, re + im)):
        hi, lo = halves(x)
        t.append(
            lax.dot_general(
                jnp.concatenate([hi, lo, hi], axis=1),
                cat_ref[v],
                NT,
                preferred_element_type=F32,
            )
        )
    return combine(t)


def store_cat(cat_ref, re, im):
    for v, x in enumerate((re, im, re + im)):
        hi, lo = halves(x)
        cat_ref[v] = jnp.concatenate([hi, hi, lo], axis=1)


def wide_product(re, im, ref):
    c_re, c_im = ref[0], ref[1]
    t = []
    for left, right in ((re, c_re), (im, c_im), (re + im, c_re + c_im)):
        a_hi, a_lo = halves(left)
        b_hi, b_lo = halves(right)
        t.append(dot_nn(a_hi, a_lo, b_hi, b_lo))
    return combine(t)


def main_kernel(
    rhs, leaf, e1, p1, c1, e2, p2, c2, p3, c3,
    y0_out, corr_out,
    rhs_v, leaf_v, e_v, p_v, c1_v, c2_v, c3_v,
    lhi, llo, yhi, ylo, pthi, ptlo,
    zt, pair_buf, rs_buf, rzz, zs, ryy, s_buf, p_buf, corr,
    g_loc, g_rs, g_full, h_mine, f_send, f_recv, z_send, z_recv, m_mine, x_send, x_recv,
    hcat, mcat, c1cat, c2cat, c3cat, stk1, tz, rz, stk2, v3,
    in_sem, send_sem, recv_sem,
):
    n = lax.axis_index("narrow")
    w = lax.axis_index("wide")
    y, c = n // 2, lax.rem(n, 2)
    x, z = w // 4, lax.rem(w, 4)
    b, xb = lax.rem(z, 2), lax.rem(x, 2)

    def dev(nn, ww):
        return {"narrow": nn, "wide": ww}

    partner = dev(n + 1 - 2 * c, w)
    sibling = dev(n, w + 1 - 2 * b)
    x_mate = dev(n, w + 4 - 8 * xb)

    def y_at(d):
        return lax.rem(y + d, 4)

    def z_at(d):
        return lax.rem(z + d, 4)

    def y_dev(d):
        return dev(2 * y_at(d) + c, w)

    def z_dev(d):
        return dev(n, x * 4 + z_at(d))

    def x_dev(d):
        return dev(n, lax.rem(x + d, 4) * 4 + z)

    flights = {}
    count = [0]

    def send(key, src, dst, device):
        idx = count[0]
        count[0] += 1
        copy = pltpu.make_async_remote_copy(
            src_ref=src, dst_ref=dst, send_sem=send_sem.at[idx], recv_sem=recv_sem.at[idx],
            device_id=device, device_id_type=MESH,
        )
        copy.start()
        flights[key] = copy

    def arrived(*key):
        flights[key].wait_recv()

    pending = {}

    def fetch(name, src, dst):
        copy = pltpu.make_async_copy(src, dst, in_sem.at[len(pending)])
        copy.start()
        pending[name] = copy

    def tile(j):
        return pl.ds(j * TILE, TILE)

    fetch("p2", p2, p_v.at[1])
    fetch("p3", p3, p_v.at[2])
    fetch("e1", e1, e_v.at[0])
    fetch("e2", e2, e_v.at[1])
    fetch("p1", p1, p_v.at[0])
    fetch("leaf", leaf, leaf_v)
    fetch("rhs0", rhs.at[:, :, tile(0)], rhs_v.at[:, :, tile(0)])
    fetch("c1", c1, c1_v)
    fetch("c2", c2.at[:, pl.ds(pl.multiple_of(x * R, R), R), :], c2_v)
    fetch("c3", c3.at[:, pl.ds(pl.multiple_of((x // 2) * R, R), R), :], c3_v)
    fetch("rhs1", rhs.at[:, :, tile(1)], rhs_v.at[:, :, tile(1)])
    fetch("rhs2", rhs.at[:, :, tile(2)], rhs_v.at[:, :, tile(2)])

    barrier = pltpu.get_barrier_semaphore()
    peers = [dev(lax.rem(n + d, 8), w) for d in range(1, 8)]
    peers += [z_dev(d) for d in range(1, 4)] + [x_dev(d) for d in range(1, 4)]
    for peer in peers:
        pl.semaphore_signal(barrier, inc=1, device_id=peer, device_id_type=MESH)

    for name in ("p2", "p3", "p1"):
        pending[name].wait()

    def prepare_projection(l, carry):
        at = pl.ds(pl.multiple_of(l * R, R), R)
        re, im = p_v[l, 0].T, p_v[l, 1].T
        for v, value in enumerate((re, -im, re - im)):
            pthi[v, at, :], ptlo[v, at, :] = halves(value)
        return carry

    lax.fori_loop(0, 3, prepare_projection, 0)

    pending["e1"].wait()
    pending["e2"].wait()
    for e, low, mats in ((0, 1, (0, 1)), (1, 2, (2,))):
        lines = pl.ds(low * R, (3 - low) * R)
        t = []
        for v, value in enumerate((e_v[e, 0], e_v[e, 1], e_v[e, 0] + e_v[e, 1])):
            hi, lo = halves(value)
            t.append(dot_nn(pthi[v, lines, :], ptlo[v, lines, :], hi, lo))
        pieces = combine(t)
        for k, m in enumerate(mats):
            for part in range(2):
                g_loc[:, 2 * m + part] = pieces[part][k * R : (k + 1) * R, :].reshape(8, 16, R)
    pl.semaphore_wait(barrier, len(peers))
    for d in range(1, 8):
        to = lax.rem(n + d, 8)
        send(("g", d), g_loc.at[to], g_rs.at[d - 1], dev(to, w))

    def sides(value, flag):
        left, right = value[:, :R], value[:, R:]
        return jnp.where(flag == 0, left, right), jnp.where(flag == 0, right, left)

    def factor_one():
        for d in range(1, 8):
            arrived("g", d)
        total = g_loc[n]
        for d in range(7):
            total = total + g_rs[d]
        for part in range(2):
            z_send[part] = total[4 + part]
        for d in (2, 1, 3):
            send(("gz", d), z_send, z_recv.at[d - 1], z_dev(d))
        pending["c1"].wait()
        both = wide_product(
            jnp.concatenate([total[0], total[2]], axis=0), jnp.concatenate([total[1], total[3]], axis=0), c1_v
        )
        for part in range(2):
            h_mine[part], f_send[part] = sides(both[part], b)
        send(("f",), f_send, f_recv, sibling)

    def factor_two():
        for d in (2, 1, 3):
            arrived("gz", d)
        total = [z_send[part] + z_recv[0, part] + z_recv[1, part] + z_recv[2, part] for part in range(2)]
        pending["c2"].wait()
        both = wide_product(total[0], total[1], c2_v)
        for part in range(2):
            m_mine[part], x_send[part] = sides(both[part], xb)
        send(("m",), x_send, x_recv, x_mate)

    def factor_three():
        arrived("f")
        arrived("m")
        for part in range(2):
            h = h_mine[part] + f_recv[part]
            g_full[n, part] = h[:16]
            g_full[n, 2 + part] = h[16:]
            g_full[n, 4 + part] = m_mine[part] + x_recv[part]
        for d in range(1, 8):
            send(("ag", d), g_full.at[n], g_full.at[n], dev(lax.rem(n + d, 8), w))

    def factor_four():
        for d in range(1, 8):
            arrived("ag", d)
        h = [jnp.concatenate([g_full[:, part].reshape(R, R), g_full[:, 2 + part].reshape(R, R)], axis=0) for part in range(2)]
        store_cat(hcat, h[0], h[1])
        store_cat(mcat, g_full[:, 4].reshape(R, R), g_full[:, 5].reshape(R, R))

    pending["leaf"].wait()

    def split_leaf(q, carry):
        at = pl.ds(pl.multiple_of(q * 128, 128), 128)
        re, im = leaf_v[0, at, :], leaf_v[1, at, :]
        for v, value in enumerate((re, im, re + im)):
            lhi[v, at, :], llo[v, at, :] = halves(value)
        return carry

    lax.fori_loop(0, 8, split_leaf, 0)
    outs = []

    def solve(j, first, last):
        def one(l, carry):
            rows = pl.ds(pl.multiple_of(l * LEAF, LEAF), LEAF)
            cols = tile(j)
            b_re, b_im = rhs_v[0, rows, cols], rhs_v[1, rows, cols]
            t = []
            for v, value in enumerate((b_re, b_im, b_re + b_im)):
                hi, lo = halves(value)
                t.append(dot_nn(lhi[v, rows, :], llo[v, rows, :], hi, lo))
            re, im = combine(t)
            rhs_v[0, rows, cols] = re
            rhs_v[1, rows, cols] = im
            for v, value in enumerate((re, im, re + im)):
                yhi[v, rows, :], ylo[v, rows, :] = halves(value)
            return carry

        lax.fori_loop(first, last, one, 0)

    def project(j):
        copy = pltpu.make_async_copy(rhs_v.at[:, :, tile(j)], y0_out.at[:, :, tile(j)], in_sem.at[12 + j])
        copy.start()
        outs.append(copy)
        t = [dot_nn(pthi[v], ptlo[v], yhi[v], ylo[v]) for v in range(3)]
        for part, value in enumerate(combine(t)):
            for l in range(3):
                zt[l, part, j] = value[l * R : (l + 1) * R, :].T.reshape(4, 2, 4, 8, R)
        send(("a", j), zt.at[:, :, j, :, 1 - c], pair_buf.at[j], partner)

    def sum_pair(j):
        arrived("a", j)
        zt[:, :, j, :, c] = zt[:, :, j, :, c] + pair_buf[j]
        for d in (2, 1, 3):
            send(("b", j, d), zt.at[0, :, j, y_at(d), c], rs_buf.at[j, d - 1], y_dev(d))
            send(("zz", j, d), zt.at[pl.ds(1, 2), :, j, :, c, z_at(d)], rzz.at[j, d - 1], z_dev(d))

    def sum_z(j):
        for d in (1, 3, 2):
            arrived("zz", j, d)
        zs[:, :, j] = zt[1:3, :, j, :, c, z] + rzz[j, 0] + rzz[j, 1] + rzz[j, 2]
        for d in (2, 1, 3):
            send(("yy", j, d), zs.at[:, :, j, y_at(d)], ryy.at[j, d - 1], y_dev(d))

    def stage_one(g, j0, nj):
        js = pl.ds(j0, nj)
        for j in range(j0, j0 + nj):
            for d in (1, 3, 2):
                arrived("b", j, d)
            s_buf[:, j] = zt[0, :, j, y, c] + rs_buf[j, 0] + rs_buf[j, 1] + rs_buf[j, 2]
        stk1[b, :, js] = s_buf[:, js]
        send(("sib", g), stk1.at[b, :, js], stk1.at[b, :, js], sibling)
        q = small_product(s_buf[0, js].reshape(nj * 32, R), s_buf[1, js].reshape(nj * 32, R), hcat)
        for part in range(2):
            for k in range(2):
                cut = q[part][:, k * R : (k + 1) * R].reshape(nj, 4, 8, R)
                for q4 in range(4):
                    tz[q4, k, part, js] = cut[:, q4]
        for d in (2, 1, 3):
            send(("rz", g, d), tz.at[z_at(d), :, :, js], rz.at[d - 1, :, :, js], z_dev(d))

    def stage_two(g, j0, nj):
        js = pl.ds(j0, nj)
        arrived("sib", g)
        pairs = [
            jnp.concatenate([stk1[p, part, js].reshape(nj * 32, R) for p in range(2)], axis=1) for part in range(2)
        ]
        k1 = small_product(pairs[0], pairs[1], c1cat)
        for part in range(2):
            corr[0, part, js, y, c] = k1[part].reshape(nj, 4, 8, R)
        block = corr.at[0, :, js, y, c]
        send(("p", g, 0), block, block, partner)
        for d in (2, 1, 3):
            send(("s", g, 0, d), block, block, y_dev(d))
        for d in (1, 3, 2):
            arrived("rz", g, d)
        for j in range(j0, j0 + nj):
            for d in (1, 3, 2):
                arrived("yy", j, d)
            total = zs[:, :, j, y] + ryy[j, 0] + ryy[j, 1] + ryy[j, 2]
            p_buf[:, :, j] = total - tz[z, :, :, j] - rz[0, :, :, j] - rz[1, :, :, j] - rz[2, :, :, j]
        stk2[xb, :, js] = p_buf[0, :, js]
        send(("xm", g), stk2.at[xb, :, js], stk2.at[xb, :, js], x_mate)
        m = small_product(p_buf[0, 0, js].reshape(nj * 8, R), p_buf[0, 1, js].reshape(nj * 8, R), mcat)
        for part in range(2):
            v3[x, part, js] = p_buf[1, part, js] - m[part].reshape(nj, 8, R)
        for d in (2, 1, 3):
            send(("v", g, d), v3.at[x, :, js], v3.at[x, :, js], x_dev(d))

    def stage_three(g, j0, nj):
        js = pl.ds(j0, nj)
        arrived("xm", g)
        pairs = [jnp.concatenate([stk2[p, part, js].reshape(nj * 8, R) for p in range(2)], axis=1) for part in range(2)]
        k2 = small_product(pairs[0], pairs[1], c2cat)
        for part in range(2):
            corr[1, part, js, y, c, z] = k2[part].reshape(nj, 8, R)
        piece = corr.at[1, :, js, y, c, z]
        for d in (2, 1, 3):
            send(("u", g, 1, d), piece, piece, z_dev(d))
        for d in (1, 3, 2):
            arrived("v", g, d)
        pairs = [
            jnp.concatenate(
                [(v3[p, part, js] + v3[p + 1, part, js]).reshape(nj * 8, R) for p in (0, 2)], axis=1
            )
            for part in range(2)
        ]
        k3 = small_product(pairs[0], pairs[1], c3cat)
        for part in range(2):
            corr[2, part, js, y, c, z] = k3[part].reshape(nj, 8, R)
        piece = corr.at[2, :, js, y, c, z]
        for d in (2, 1, 3):
            send(("u", g, 2, d), piece, piece, y_dev(d))

    def forward_y(g, l, j0, nj):
        js = pl.ds(j0, nj)
        for d in (1, 3, 2):
            arrived("s", g, l, d)
            block = corr.at[l, :, js, y_at(4 - d), c]
            send(("f", g, l, d), block, block, partner)

    def stage_four(g, j0, nj):
        js = pl.ds(j0, nj)
        for l, block, to in (
            (1, corr.at[1, :, js, y, c], y_dev),
            (2, corr.at[2, :, js, :, c, z], z_dev),
        ):
            for d in (1, 3, 2):
                arrived("u", g, l, d)
            for d in (2, 1, 3):
                send(("s", g, l, d), block, block, to(d))
            send(("p", g, l), block, block, partner)

    def stage_five(g, j0, nj):
        js = pl.ds(j0, nj)
        forward_y(g, 1, j0, nj)
        for d in (1, 3, 2):
            arrived("s", g, 2, d)
            block = corr.at[2, :, js, :, c, z_at(4 - d)]
            send(("f", g, 2, d), block, block, partner)

    def stage_six(g, j0, nj):
        for l in range(3):
            arrived("p", g, l)
            for d in (1, 3, 2):
                arrived("f", g, l, d)
        js = pl.ds(j0, nj)
        copy = pltpu.make_async_copy(corr.at[:, :, js], corr_out.at[:, :, js], in_sem.at[15 + g])
        copy.start()
        outs.append(copy)

    first, last = (0, 0, 2), (1, 2, 1)
    pending["rhs0"].wait()
    solve(0, 0, 2)
    factor_one()
    project(0)
    factor_two()
    pending["rhs1"].wait()
    solve(1, 0, 1)
    sum_pair(0)
    solve(1, 1, 2)
    factor_three()
    project(1)
    sum_z(0)
    pending["rhs2"].wait()
    solve(2, 0, 1)
    sum_pair(1)
    solve(2, 1, 2)
    sum_z(1)
    project(2)
    pending["c3"].wait()
    store_cat(c1cat, c1_v[0], c1_v[1])
    store_cat(c2cat, c2_v[0], c2_v[1])
    store_cat(c3cat, c3_v[0], c3_v[1])
    sum_pair(2)
    factor_four()
    stage_one(*first)
    sum_z(2)
    stage_two(*first)
    stage_one(*last)
    stage_three(*first)
    forward_y(*first[:1], 0, *first[1:])
    stage_two(*last)
    stage_four(*first)
    stage_three(*last)
    stage_five(*first)
    forward_y(*last[:1], 0, *last[1:])
    stage_four(*last)
    stage_six(*first)
    stage_five(*last)
    stage_six(*last)

    for copy in flights.values():
        copy.wait_send()
    for copy in outs:
        copy.wait()


def main_call(rhs, leaf, e1, p1, c1, e2, p2, c2, p3, c3):
    any_spec = pl.BlockSpec(memory_space=pl.ANY)
    vm = pltpu.VMEM
    return pl.pallas_call(
        main_kernel,
        out_shape=(
            jax.ShapeDtypeStruct((2, ROWS, NR), F32),
            jax.ShapeDtypeStruct((3, 2, 3, 4, 2, 4, 8, R), F32),
        ),
        in_specs=[any_spec] * 10,
        out_specs=(any_spec, any_spec),
        scratch_shapes=[
            vm((2, ROWS, NR), F32),
            vm((2, ROWS, LEAF), F32),
            vm((2, 2, ROWS, R), F32),
            vm((3, 2, ROWS, R), F32),
            vm((2, R, 2 * R), F32),
            vm((2, R, 2 * R), F32),
            vm((2, R, 2 * R), F32),
            vm((3, ROWS, LEAF), BF16),
            vm((3, ROWS, LEAF), BF16),
            vm((3, ROWS, TILE), BF16),
            vm((3, ROWS, TILE), BF16),
            vm((3, 3 * R, ROWS), BF16),
            vm((3, 3 * R, ROWS), BF16),
            vm((3, 2, 3, 4, 2, 4, 8, R), F32),
            vm((3, 3, 2, 4, 4, 8, R), F32),
            vm((3, 3, 2, 4, 8, R), F32),
            vm((3, 3, 2, 2, 4, 8, R), F32),
            vm((2, 2, 3, 4, 8, R), F32),
            vm((3, 3, 2, 2, 8, R), F32),
            vm((2, 3, 4, 8, R), F32),
            vm((2, 2, 3, 8, R), F32),
            vm((3, 2, 3, 4, 2, 4, 8, R), F32),
            vm((8, 6, 16, R), F32),
            vm((7, 6, 16, R), F32),
            vm((8, 6, 16, R), F32),
            vm((2, 32, R), F32),
            vm((2, 32, R), F32),
            vm((2, 32, R), F32),
            vm((2, 16, R), F32),
            vm((3, 2, 16, R), F32),
            vm((2, 16, R), F32),
            vm((2, 16, R), F32),
            vm((2, 16, R), F32),
            vm((3, 2 * R, 3 * R), BF16),
            vm((3, R, 3 * R), BF16),
            vm((3, R, 6 * R), BF16),
            vm((3, R, 6 * R), BF16),
            vm((3, R, 6 * R), BF16),
            vm((2, 2, 3, 4, 8, R), F32),
            vm((4, 2, 2, 3, 8, R), F32),
            vm((3, 2, 2, 3, 8, R), F32),
            vm((2, 2, 3, 8, R), F32),
            vm((4, 2, 3, 8, R), F32),
            pltpu.SemaphoreType.DMA((17,)),
            pltpu.SemaphoreType.DMA((NSEM,)),
            pltpu.SemaphoreType.DMA((NSEM,)),
        ],
        compiler_params=pltpu.CompilerParams(
            collective_id=0, has_side_effects=True, vmem_limit_bytes=60 * 1024 * 1024
        ),
        cost_estimate=pl.CostEstimate(flops=14_000_000_000, bytes_accessed=26_000_000, transcendentals=0),
    )(rhs, leaf, e1, p1, c1, e2, p2, c2, p3, c3)


def expand_kernel(y0, e1, e2, e3, corr, out, chi, clo):
    @pl.when(pl.program_id(0) == 0)
    def _():
        for l in range(3):
            lanes = slice(l * R, (l + 1) * R)
            re, im = corr[l, 0], corr[l, 1]
            for v, value in enumerate((re, im, re + im)):
                chi[v, :, lanes], clo[v, :, lanes] = halves(value)

    e_re = jnp.concatenate([e1[0], e2[0], e3[0]], axis=1)
    e_im = jnp.concatenate([e1[1], e2[1], e3[1]], axis=1)
    t = []
    for v, value in enumerate((e_re, e_im, e_re + e_im)):
        hi, lo = halves(value)
        t.append(
            lax.dot_general(
                jnp.concatenate([hi, lo, hi], axis=1),
                jnp.concatenate([chi[v], chi[v], clo[v]], axis=1),
                NT,
                preferred_element_type=F32,
            )
        )
    re, im = combine(t)
    out[0] = y0[0] - re
    out[1] = y0[1] - im


def expand_call(y0, e1, e2, e3, corr):
    tm = 256
    rows = pl.BlockSpec((2, tm, NR), lambda i: (0, i, 0))
    base = pl.BlockSpec((2, tm, R), lambda i: (0, i, 0))
    return pl.pallas_call(
        expand_kernel,
        out_shape=jax.ShapeDtypeStruct((2, ROWS, NR), F32),
        grid=(ROWS // tm,),
        in_specs=[rows, base, base, base, pl.BlockSpec((3, 2, NR, R), lambda i: (0, 0, 0, 0))],
        out_specs=rows,
        scratch_shapes=[pltpu.VMEM((3, NR, 3 * R), BF16), pltpu.VMEM((3, NR, 3 * R), BF16)],
        compiler_params=pltpu.CompilerParams(
            dimension_semantics=("arbitrary",), vmem_limit_bytes=48 * 1024 * 1024
        ),
        cost_estimate=pl.CostEstimate(flops=5_400_000_000, bytes_accessed=18_000_000, transcendentals=0),
    )(y0, e1, e2, e3, corr)


def body(rhs, leaf, e1, p1, c1, e2, p2, c2, e3, p3, c3):
    y0, corr = main_call(rhs, leaf, e1, p1, c1, e2, p2, c2, p3, c3)
    return expand_call(y0, e1, e2, e3, corr.reshape(3, 2, NR, R))


def solution(mesh):
    split = P(None, ("wide", "narrow"), None)
    placed = (split, split, split, split, P(None, "wide", None), split, split, P(), split, split, P())
    return jax.shard_map(body, mesh=mesh, in_specs=placed, out_specs=split, check_vma=False)
```

```python
import functools

import jax
import jax.numpy as jnp
from jax import lax
from jax.experimental import pallas as pl
from jax.experimental.pallas import tpu as pltpu
from jax.sharding import PartitionSpec as P

MESH = pl.DeviceIdType.MESH
F32 = jnp.float32
BF16 = jnp.bfloat16
LEAF = 512
R = 128
NR = 768
ROWS = 1024
TILE = 256
NSEM = 120
NT = (((1,), (1,)), ((), ()))


def halves(x):
    hi = x.astype(BF16)
    return hi, (x - hi.astype(F32)).astype(BF16)


def dot_nn(a_hi, a_lo, b_hi, b_lo):
    a = jnp.concatenate([a_hi, a_lo, a_hi], axis=1)
    b = jnp.concatenate([b_hi, b_hi, b_lo], axis=0)
    return jnp.dot(a, b, preferred_element_type=F32)


def dot_nt(a_hi, a_lo, b_hi, b_lo):
    a = jnp.concatenate([a_hi, a_lo, a_hi], axis=1)
    b = jnp.concatenate([b_hi, b_hi, b_lo], axis=1)
    return lax.dot_general(a, b, NT, preferred_element_type=F32)


def combine(t):
    return t[0] - t[1], t[2] - t[0] - t[1]


def small_product(re, im, cat_ref):
    t = []
    for v, x in enumerate((re, im, re + im)):
        hi, lo = halves(x)
        t.append(
            lax.dot_general(
                jnp.concatenate([hi, lo, hi], axis=1),
                cat_ref[v],
                NT,
                preferred_element_type=F32,
            )
        )
    return combine(t)


def store_cat(cat_ref, re, im):
    for v, x in enumerate((re, im, re + im)):
        hi, lo = halves(x)
        cat_ref[v] = jnp.concatenate([hi, hi, lo], axis=1)


def wide_product(re, im, ref):
    c_re, c_im = ref[0], ref[1]
    t = []
    for left, right in ((re, c_re), (im, c_im), (re + im, c_re + c_im)):
        a_hi, a_lo = halves(left)
        b_hi, b_lo = halves(right)
        t.append(dot_nn(a_hi, a_lo, b_hi, b_lo))
    return combine(t)


def main_kernel(
    rhs, leaf, e1, p1, c1, e2, p2, c2, e3, p3, c3,
    y_out, corr_out,
    rhs_v, leaf_v, e_v, p_v, c1_v, c2_v, c3_v,
    lhi, llo, yhi, ylo, pthi, ptlo,
    zt, pair_buf, rs_buf, rzz, zs, ryy, s_buf, p_buf, corr,
    g_loc, g_rs, g_full, h_mine, f_send, f_recv, z_send, z_recv, m_mine, x_send, x_recv,
    ehi, elo, chi, clo, hcat, mcat, c1cat, c2cat, c3cat, stk1, tz, rz, stk2, v3,
    in_sem, send_sem, recv_sem,
):
    n = lax.axis_index("narrow")
    w = lax.axis_index("wide")
    y, c = n // 2, lax.rem(n, 2)
    x, z = w // 4, lax.rem(w, 4)
    b, xb = lax.rem(z, 2), lax.rem(x, 2)

    def dev(nn, ww):
        return {"narrow": nn, "wide": ww}

    partner = dev(n + 1 - 2 * c, w)
    sibling = dev(n, w + 1 - 2 * b)
    x_mate = dev(n, w + 4 - 8 * xb)

    def y_at(d):
        return lax.rem(y + d, 4)

    def z_at(d):
        return lax.rem(z + d, 4)

    def y_dev(d):
        return dev(2 * y_at(d) + c, w)

    def z_dev(d):
        return dev(n, x * 4 + z_at(d))

    def x_dev(d):
        return dev(n, lax.rem(x + d, 4) * 4 + z)

    flights = {}
    count = [0]

    def send(key, src, dst, device):
        idx = count[0]
        count[0] += 1
        copy = pltpu.make_async_remote_copy(
            src_ref=src, dst_ref=dst, send_sem=send_sem.at[idx], recv_sem=recv_sem.at[idx],
            device_id=device, device_id_type=MESH,
        )
        copy.start()
        flights[key] = copy

    def arrived(*key):
        flights[key].wait_recv()

    pending = {}

    def fetch(name, src, dst):
        copy = pltpu.make_async_copy(src, dst, in_sem.at[len(pending)])
        copy.start()
        pending[name] = copy

    def tile(j):
        return pl.ds(j * TILE, TILE)

    fetch("p2", p2, p_v.at[1])
    fetch("p3", p3, p_v.at[2])
    fetch("e1", e1, e_v.at[0])
    fetch("e2", e2, e_v.at[1])
    fetch("p1", p1, p_v.at[0])
    fetch("leaf", leaf, leaf_v)
    fetch("rhs0", rhs.at[:, :, tile(0)], rhs_v.at[:, :, tile(0)])
    fetch("c1", c1, c1_v)
    fetch("c2", c2.at[:, pl.ds(pl.multiple_of(x * R, R), R), :], c2_v)
    fetch("c3", c3.at[:, pl.ds(pl.multiple_of((x // 2) * R, R), R), :], c3_v)
    fetch("e3", e3, e_v.at[2])
    fetch("rhs1", rhs.at[:, :, tile(1)], rhs_v.at[:, :, tile(1)])
    fetch("rhs2", rhs.at[:, :, tile(2)], rhs_v.at[:, :, tile(2)])

    barrier = pltpu.get_barrier_semaphore()
    peers = [dev(lax.rem(n + d, 8), w) for d in range(1, 8)]
    peers += [z_dev(d) for d in range(1, 4)] + [x_dev(d) for d in range(1, 4)]
    for peer in peers:
        pl.semaphore_signal(barrier, inc=1, device_id=peer, device_id_type=MESH)

    for name in ("p2", "p3"):
        pending[name].wait()

    def prepare_projection(l, carry):
        at = pl.ds(pl.multiple_of(l * R, R), R)
        re, im = p_v[l, 0].T, p_v[l, 1].T
        for v, value in enumerate((re, -im, re - im)):
            pthi[v, at, :], ptlo[v, at, :] = halves(value)
        return carry

    lax.fori_loop(1, 3, prepare_projection, 0)

    pending["e1"].wait()
    pending["e2"].wait()
    for e, low, mats in ((0, 1, (0, 1)), (1, 2, (2,))):
        lines = pl.ds(low * R, (3 - low) * R)
        t = []
        for v, value in enumerate((e_v[e, 0], e_v[e, 1], e_v[e, 0] + e_v[e, 1])):
            hi, lo = halves(value)
            t.append(dot_nn(pthi[v, lines, :], ptlo[v, lines, :], hi, lo))
        pieces = combine(t)
        for k, m in enumerate(mats):
            for part in range(2):
                g_loc[:, 2 * m + part] = pieces[part][k * R : (k + 1) * R, :].reshape(8, 16, R)
    pl.semaphore_wait(barrier, len(peers))
    for d in range(1, 8):
        to = lax.rem(n + d, 8)
        send(("g", d), g_loc.at[to], g_rs.at[d - 1], dev(to, w))

    def sides(value, flag):
        left, right = value[:, :R], value[:, R:]
        return jnp.where(flag == 0, left, right), jnp.where(flag == 0, right, left)

    def factor_one():
        for d in range(1, 8):
            arrived("g", d)
        total = g_loc[n]
        for d in range(7):
            total = total + g_rs[d]
        for part in range(2):
            z_send[part] = total[4 + part]
        for d in (2, 1, 3):
            send(("gz", d), z_send, z_recv.at[d - 1], z_dev(d))
        pending["c1"].wait()
        both = wide_product(
            jnp.concatenate([total[0], total[2]], axis=0), jnp.concatenate([total[1], total[3]], axis=0), c1_v
        )
        for part in range(2):
            h_mine[part], f_send[part] = sides(both[part], b)
        send(("f",), f_send, f_recv, sibling)

    def factor_two():
        for d in (2, 1, 3):
            arrived("gz", d)
        total = [z_send[part] + z_recv[0, part] + z_recv[1, part] + z_recv[2, part] for part in range(2)]
        pending["c2"].wait()
        both = wide_product(total[0], total[1], c2_v)
        for part in range(2):
            m_mine[part], x_send[part] = sides(both[part], xb)
        send(("m",), x_send, x_recv, x_mate)

    def factor_three():
        arrived("f")
        arrived("m")
        for part in range(2):
            h = h_mine[part] + f_recv[part]
            g_full[n, part] = h[:16]
            g_full[n, 2 + part] = h[16:]
            g_full[n, 4 + part] = m_mine[part] + x_recv[part]
        for d in range(1, 8):
            send(("ag", d), g_full.at[n], g_full.at[n], dev(lax.rem(n + d, 8), w))

    def factor_four():
        for d in range(1, 8):
            arrived("ag", d)
        h = [jnp.concatenate([g_full[:, part].reshape(R, R), g_full[:, 2 + part].reshape(R, R)], axis=0) for part in range(2)]
        store_cat(hcat, h[0], h[1])
        store_cat(mcat, g_full[:, 4].reshape(R, R), g_full[:, 5].reshape(R, R))

    pending["p1"].wait()
    prepare_projection(0, 0)
    pending["leaf"].wait()

    def split_leaf(q, carry):
        at = pl.ds(pl.multiple_of(q * 128, 128), 128)
        re, im = leaf_v[0, at, :], leaf_v[1, at, :]
        for v, value in enumerate((re, im, re + im)):
            lhi[v, at, :], llo[v, at, :] = halves(value)
        return carry

    lax.fori_loop(0, 8, split_leaf, 0)
    outs = []

    def solve(j, first, last):
        def one(l, carry):
            rows = pl.ds(pl.multiple_of(l * LEAF, LEAF), LEAF)
            cols = tile(j)
            b_re, b_im = rhs_v[0, rows, cols], rhs_v[1, rows, cols]
            t = []
            for v, value in enumerate((b_re, b_im, b_re + b_im)):
                hi, lo = halves(value)
                t.append(dot_nn(lhi[v, rows, :], llo[v, rows, :], hi, lo))
            re, im = combine(t)
            rhs_v[0, rows, cols] = re
            rhs_v[1, rows, cols] = im
            for v, value in enumerate((re, im, re + im)):
                yhi[v, rows, :], ylo[v, rows, :] = halves(value)
            return carry

        lax.fori_loop(first, last, one, 0)

    def project(j):
        t = [dot_nn(pthi[v], ptlo[v], yhi[v], ylo[v]) for v in range(3)]
        for part, value in enumerate(combine(t)):
            for l in range(3):
                zt[l, part, j] = value[l * R : (l + 1) * R, :].T.reshape(4, 2, 4, 8, R)
        send(("a", j), zt.at[:, :, j, :, 1 - c], pair_buf.at[j], partner)

    def sum_pair(j):
        arrived("a", j)
        zt[:, :, j, :, c] = zt[:, :, j, :, c] + pair_buf[j]
        for d in (2, 1, 3):
            send(("b", j, d), zt.at[0, :, j, y_at(d), c], rs_buf.at[j, d - 1], y_dev(d))
            send(("zz", j, d), zt.at[pl.ds(1, 2), :, j, :, c, z_at(d)], rzz.at[j, d - 1], z_dev(d))

    def sum_z(j):
        for d in (1, 3, 2):
            arrived("zz", j, d)
        zs[:, :, j] = zt[1:3, :, j, :, c, z] + rzz[j, 0] + rzz[j, 1] + rzz[j, 2]
        for d in (2, 1, 3):
            send(("yy", j, d), zs.at[:, :, j, y_at(d)], ryy.at[j, d - 1], y_dev(d))

    def stage_one(g, j0, nj):
        js = pl.ds(j0, nj)
        for j in range(j0, j0 + nj):
            for d in (1, 3, 2):
                arrived("b", j, d)
            s_buf[:, j] = zt[0, :, j, y, c] + rs_buf[j, 0] + rs_buf[j, 1] + rs_buf[j, 2]
        stk1[b, :, js] = s_buf[:, js]
        send(("sib", g), stk1.at[b, :, js], stk1.at[b, :, js], sibling)
        q = small_product(s_buf[0, js].reshape(nj * 32, R), s_buf[1, js].reshape(nj * 32, R), hcat)
        for part in range(2):
            for k in range(2):
                cut = q[part][:, k * R : (k + 1) * R].reshape(nj, 4, 8, R)
                for q4 in range(4):
                    tz[q4, k, part, js] = cut[:, q4]
        for d in (2, 1, 3):
            send(("rz", g, d), tz.at[z_at(d), :, :, js], rz.at[d - 1, :, :, js], z_dev(d))

    def stage_two(g, j0, nj):
        js = pl.ds(j0, nj)
        arrived("sib", g)
        pairs = [
            jnp.concatenate([stk1[p, part, js].reshape(nj * 32, R) for p in range(2)], axis=1) for part in range(2)
        ]
        k1 = small_product(pairs[0], pairs[1], c1cat)
        for part in range(2):
            corr[0, part, js, y, c] = k1[part].reshape(nj, 4, 8, R)
        block = corr.at[0, :, js, y, c]
        send(("p", g, 0), block, block, partner)
        for d in (2, 1, 3):
            send(("s", g, 0, d), block, block, y_dev(d))
        for d in (1, 3, 2):
            arrived("rz", g, d)
        for j in range(j0, j0 + nj):
            for d in (1, 3, 2):
                arrived("yy", j, d)
            total = zs[:, :, j, y] + ryy[j, 0] + ryy[j, 1] + ryy[j, 2]
            p_buf[:, :, j] = total - tz[z, :, :, j] - rz[0, :, :, j] - rz[1, :, :, j] - rz[2, :, :, j]
        stk2[xb, :, js] = p_buf[0, :, js]
        send(("xm", g), stk2.at[xb, :, js], stk2.at[xb, :, js], x_mate)
        m = small_product(p_buf[0, 0, js].reshape(nj * 8, R), p_buf[0, 1, js].reshape(nj * 8, R), mcat)
        for part in range(2):
            v3[x, part, js] = p_buf[1, part, js] - m[part].reshape(nj, 8, R)
        for d in (2, 1, 3):
            send(("v", g, d), v3.at[x, :, js], v3.at[x, :, js], x_dev(d))

    def stage_three(g, j0, nj):
        js = pl.ds(j0, nj)
        arrived("xm", g)
        pairs = [jnp.concatenate([stk2[p, part, js].reshape(nj * 8, R) for p in range(2)], axis=1) for part in range(2)]
        k2 = small_product(pairs[0], pairs[1], c2cat)
        for part in range(2):
            corr[1, part, js, y, c, z] = k2[part].reshape(nj, 8, R)
        piece = corr.at[1, :, js, y, c, z]
        for d in (2, 1, 3):
            send(("u", g, 1, d), piece, piece, z_dev(d))
        for d in (1, 3, 2):
            arrived("v", g, d)
        pairs = [
            jnp.concatenate(
                [(v3[p, part, js] + v3[p + 1, part, js]).reshape(nj * 8, R) for p in (0, 2)], axis=1
            )
            for part in range(2)
        ]
        k3 = small_product(pairs[0], pairs[1], c3cat)
        for part in range(2):
            corr[2, part, js, y, c, z] = k3[part].reshape(nj, 8, R)
        piece = corr.at[2, :, js, y, c, z]
        for d in (2, 1, 3):
            send(("u", g, 2, d), piece, piece, y_dev(d))

    def forward_y(g, l, j0, nj):
        js = pl.ds(j0, nj)
        for d in (1, 3, 2):
            arrived("s", g, l, d)
            block = corr.at[l, :, js, y_at(4 - d), c]
            send(("f", g, l, d), block, block, partner)

    def stage_four(g, j0, nj):
        js = pl.ds(j0, nj)
        for l, block, to in (
            (1, corr.at[1, :, js, y, c], y_dev),
            (2, corr.at[2, :, js, :, c, z], z_dev),
        ):
            for d in (1, 3, 2):
                arrived("u", g, l, d)
            for d in (2, 1, 3):
                send(("s", g, l, d), block, block, to(d))
            send(("p", g, l), block, block, partner)

    def stage_five(g, j0, nj):
        js = pl.ds(j0, nj)
        forward_y(g, 1, j0, nj)
        for d in (1, 3, 2):
            arrived("s", g, 2, d)
            block = corr.at[2, :, js, :, c, z_at(4 - d)]
            send(("f", g, 2, d), block, block, partner)

    def stage_six(g, j0, nj):
        for l in range(3):
            arrived("p", g, l)
            for d in (1, 3, 2):
                arrived("f", g, l, d)
    def write(j):
        copy = pltpu.make_async_copy(rhs_v.at[:, :, tile(j)], y_out.at[:, :, tile(j)], in_sem.at[13 + j])
        copy.start()
        outs.append(copy)

    def prepare_expansion():
        pending["e3"].wait()

        def one(q, carry):
            at = pl.ds(pl.multiple_of(q * 256, 256), 256)
            for l in range(3):
                re, im = e_v[l, 0, at, :], e_v[l, 1, at, :]
                for v, value in enumerate((re, im, re + im)):
                    ehi[v, at, l * R : (l + 1) * R], elo[v, at, l * R : (l + 1) * R] = halves(value)
            return carry

        lax.fori_loop(0, 4, one, 0)

    def expand(j, start, stop):
        cols = tile(j)
        if start == 0:
            for l in range(3):
                lanes = slice(l * R, (l + 1) * R)
                re, im = corr[l, 0, j].reshape(TILE, R), corr[l, 1, j].reshape(TILE, R)
                for v, value in enumerate((re, im, re + im)):
                    chi[v, :, lanes], clo[v, :, lanes] = halves(value)

        def one(q, carry):
            rows = pl.ds(pl.multiple_of(q * 512, 512), 512)
            re, im = combine([dot_nt(ehi[v, rows, :], elo[v, rows, :], chi[v], clo[v]) for v in range(3)])
            rhs_v[0, rows, cols] = rhs_v[0, rows, cols] - re
            rhs_v[1, rows, cols] = rhs_v[1, rows, cols] - im
            return carry

        lax.fori_loop(start, stop, one, 0)

    first, last = (0, 0, 2), (1, 2, 1)
    pending["rhs0"].wait()
    solve(0, 0, 2)
    project(0)
    factor_one()
    pending["rhs1"].wait()
    solve(1, 0, 1)
    sum_pair(0)
    solve(1, 1, 2)
    factor_two()
    project(1)
    sum_z(0)
    pending["rhs2"].wait()
    solve(2, 0, 1)
    sum_pair(1)
    factor_three()
    solve(2, 1, 2)
    sum_z(1)
    project(2)
    write(2)
    pending["c3"].wait()
    store_cat(c1cat, c1_v[0], c1_v[1])
    store_cat(c2cat, c2_v[0], c2_v[1])
    store_cat(c3cat, c3_v[0], c3_v[1])
    sum_pair(2)
    factor_four()
    stage_one(*first)
    prepare_expansion()
    sum_z(2)
    stage_two(*first)
    stage_one(*last)
    stage_three(*first)
    stage_two(*last)
    forward_y(*first[:1], 0, *first[1:])
    stage_four(*first)
    stage_three(*last)
    stage_five(*first)
    forward_y(*last[:1], 0, *last[1:])
    stage_six(*first)
    stage_four(*last)
    expand(0, 0, 2)
    write(0)
    stage_five(*last)
    expand(1, 0, 1)
    stage_six(*last)
    copy = pltpu.make_async_copy(corr.at[:, :, 2], corr_out, in_sem.at[16])
    copy.start()
    outs.append(copy)
    expand(1, 1, 2)
    write(1)

    for copy in flights.values():
        copy.wait_send()
    for copy in outs:
        copy.wait()


def main_call(rhs, leaf, e1, p1, c1, e2, p2, c2, e3, p3, c3):
    any_spec = pl.BlockSpec(memory_space=pltpu.HBM)
    vm = pltpu.VMEM
    return pl.pallas_call(
        main_kernel,
        out_shape=(
            jax.ShapeDtypeStruct((2, ROWS, NR), F32),
            jax.ShapeDtypeStruct((3, 2, 4, 2, 4, 8, R), F32),
        ),
        in_specs=[any_spec] * 11,
        out_specs=(any_spec, any_spec),
        scratch_shapes=[
            vm((2, ROWS, NR), F32),
            vm((2, ROWS, LEAF), F32),
            vm((3, 2, ROWS, R), F32),
            vm((3, 2, ROWS, R), F32),
            vm((2, R, 2 * R), F32),
            vm((2, R, 2 * R), F32),
            vm((2, R, 2 * R), F32),
            vm((3, ROWS, LEAF), BF16),
            vm((3, ROWS, LEAF), BF16),
            vm((3, ROWS, TILE), BF16),
            vm((3, ROWS, TILE), BF16),
            vm((3, 3 * R, ROWS), BF16),
            vm((3, 3 * R, ROWS), BF16),
            vm((3, 2, 3, 4, 2, 4, 8, R), F32),
            vm((3, 3, 2, 4, 4, 8, R), F32),
            vm((3, 3, 2, 4, 8, R), F32),
            vm((3, 3, 2, 2, 4, 8, R), F32),
            vm((2, 2, 3, 4, 8, R), F32),
            vm((3, 3, 2, 2, 8, R), F32),
            vm((2, 3, 4, 8, R), F32),
            vm((2, 2, 3, 8, R), F32),
            vm((3, 2, 3, 4, 2, 4, 8, R), F32),
            vm((8, 6, 16, R), F32),
            vm((7, 6, 16, R), F32),
            vm((8, 6, 16, R), F32),
            vm((2, 32, R), F32),
            vm((2, 32, R), F32),
            vm((2, 32, R), F32),
            vm((2, 16, R), F32),
            vm((3, 2, 16, R), F32),
            vm((2, 16, R), F32),
            vm((2, 16, R), F32),
            vm((2, 16, R), F32),
            vm((3, ROWS, 3 * R), BF16),
            vm((3, ROWS, 3 * R), BF16),
            vm((3, TILE, 3 * R), BF16),
            vm((3, TILE, 3 * R), BF16),
            vm((3, 2 * R, 3 * R), BF16),
            vm((3, R, 3 * R), BF16),
            vm((3, R, 6 * R), BF16),
            vm((3, R, 6 * R), BF16),
            vm((3, R, 6 * R), BF16),
            vm((2, 2, 3, 4, 8, R), F32),
            vm((4, 2, 2, 3, 8, R), F32),
            vm((3, 2, 2, 3, 8, R), F32),
            vm((2, 2, 3, 8, R), F32),
            vm((4, 2, 3, 8, R), F32),
            pltpu.SemaphoreType.DMA((17,)),
            pltpu.SemaphoreType.DMA((NSEM,)),
            pltpu.SemaphoreType.DMA((NSEM,)),
        ],
        compiler_params=pltpu.CompilerParams(
            collective_id=0, has_side_effects=True, vmem_limit_bytes=60 * 1024 * 1024
        ),
        cost_estimate=pl.CostEstimate(flops=14_000_000_000, bytes_accessed=26_000_000, transcendentals=0),
    )(rhs, leaf, e1, p1, c1, e2, p2, c2, e3, p3, c3)


def expand_kernel(y, e1, e2, e3, corr, out, chi, clo):
    @pl.when(pl.program_id(0) == 0)
    def _():
        for l in range(3):
            lanes = slice(l * R, (l + 1) * R)
            re, im = corr[l, 0], corr[l, 1]
            for v, value in enumerate((re, im, re + im)):
                chi[v, :, lanes], clo[v, :, lanes] = halves(value)

    done = NR - TILE
    out[:, :, :done] = y[:, :, :done]
    e_re = jnp.concatenate([e1[0], e2[0], e3[0]], axis=1)
    e_im = jnp.concatenate([e1[1], e2[1], e3[1]], axis=1)
    t = []
    for v, value in enumerate((e_re, e_im, e_re + e_im)):
        hi, lo = halves(value)
        t.append(dot_nt(hi, lo, chi[v], clo[v]))
    re, im = combine(t)
    out[0, :, done:] = y[0, :, done:] - re
    out[1, :, done:] = y[1, :, done:] - im


def expand_call(y, e1, e2, e3, corr):
    tm = 256
    rows = pl.BlockSpec((2, tm, NR), lambda i: (0, i, 0))
    base = pl.BlockSpec((2, tm, R), lambda i: (0, i, 0))
    return pl.pallas_call(
        expand_kernel,
        out_shape=jax.ShapeDtypeStruct((2, ROWS, NR), F32),
        grid=(ROWS // tm,),
        in_specs=[rows, base, base, base, pl.BlockSpec((3, 2, TILE, R), lambda i: (0, 0, 0, 0))],
        out_specs=rows,
        scratch_shapes=[pltpu.VMEM((3, TILE, 3 * R), BF16), pltpu.VMEM((3, TILE, 3 * R), BF16)],
        compiler_params=pltpu.CompilerParams(
            dimension_semantics=("arbitrary",), vmem_limit_bytes=32 * 1024 * 1024
        ),
        cost_estimate=pl.CostEstimate(flops=5_400_000_000, bytes_accessed=18_000_000, transcendentals=0),
    )(y, e1, e2, e3, corr)


def body(rhs, leaf, e1, p1, c1, e2, p2, c2, e3, p3, c3):
    y, corr = main_call(rhs, leaf, e1, p1, c1, e2, p2, c2, e3, p3, c3)
    held = [pltpu.with_memory_space_constraint(a, pltpu.HBM) for a in (y, e1, e2, e3, corr.reshape(3, 2, TILE, R))]
    return expand_call(*held)


def solution(mesh):
    split = P(None, ("wide", "narrow"), None)
    placed = (split, split, split, split, P(None, "wide", None), split, split, P(), split, split, P())
    return jax.shard_map(body, mesh=mesh, in_specs=placed, out_specs=split, check_vma=False)
```

```python
import functools

import jax
import jax.numpy as jnp
from jax import lax
from jax.experimental import pallas as pl
from jax.experimental.pallas import tpu as pltpu
from jax.sharding import PartitionSpec as P

MESH = pl.DeviceIdType.MESH
F32 = jnp.float32
BF16 = jnp.bfloat16
LEAF = 512
R = 128
NR = 768
ROWS = 1024
TILE = 256
NSEM = 120
NT = (((1,), (1,)), ((), ()))


def halves(x):
    hi = x.astype(BF16)
    return hi, (x - hi.astype(F32)).astype(BF16)


def dot_nn(a_hi, a_lo, b_hi, b_lo):
    a = jnp.concatenate([a_hi, a_lo, a_hi], axis=1)
    b = jnp.concatenate([b_hi, b_hi, b_lo], axis=0)
    return jnp.dot(a, b, preferred_element_type=F32)


def dot_nt(a_hi, a_lo, b_hi, b_lo):
    a = jnp.concatenate([a_hi, a_lo, a_hi], axis=1)
    b = jnp.concatenate([b_hi, b_hi, b_lo], axis=1)
    return lax.dot_general(a, b, NT, preferred_element_type=F32)


def combine(t):
    return t[0] - t[1], t[2] - t[0] - t[1]


def small_product(re, im, cat_ref):
    t = []
    for v, x in enumerate((re, im, re + im)):
        hi, lo = halves(x)
        t.append(
            lax.dot_general(
                jnp.concatenate([hi, lo, hi], axis=1),
                cat_ref[v],
                NT,
                preferred_element_type=F32,
            )
        )
    return combine(t)


def store_cat(cat_ref, re, im):
    for v, x in enumerate((re, im, re + im)):
        hi, lo = halves(x)
        cat_ref[v] = jnp.concatenate([hi, hi, lo], axis=1)


def wide_product(re, im, ref):
    c_re, c_im = ref[0], ref[1]
    t = []
    for left, right in ((re, c_re), (im, c_im), (re + im, c_re + c_im)):
        a_hi, a_lo = halves(left)
        b_hi, b_lo = halves(right)
        t.append(dot_nn(a_hi, a_lo, b_hi, b_lo))
    return combine(t)


def main_kernel(
    rhs, leaf, e1, p1, c1, e2, p2, c2, e3, p3, c3,
    rhs_v, ehi, elo, corr_out,
    leaf_v, e_v, p_v, c1_v, c2_v, c3_v,
    lhi, llo, yhi, ylo, pthi, ptlo,
    zt, pair_buf, rs_buf, rzz, zs, ryy, s_buf, p_buf, corr,
    g_loc, g_rs, g_full, h_mine, f_send, f_recv, z_send, z_recv, m_mine, x_send, x_recv,
    chi, clo, hcat, mcat, c1cat, c2cat, c3cat, stk1, tz, rz, stk2, v3,
    in_sem, send_sem, recv_sem,
):
    n = lax.axis_index("narrow")
    w = lax.axis_index("wide")
    y, c = n // 2, lax.rem(n, 2)
    x, z = w // 4, lax.rem(w, 4)
    b, xb = lax.rem(z, 2), lax.rem(x, 2)

    def dev(nn, ww):
        return {"narrow": nn, "wide": ww}

    partner = dev(n + 1 - 2 * c, w)
    sibling = dev(n, w + 1 - 2 * b)
    x_mate = dev(n, w + 4 - 8 * xb)

    def y_at(d):
        return lax.rem(y + d, 4)

    def z_at(d):
        return lax.rem(z + d, 4)

    def y_dev(d):
        return dev(2 * y_at(d) + c, w)

    def z_dev(d):
        return dev(n, x * 4 + z_at(d))

    def x_dev(d):
        return dev(n, lax.rem(x + d, 4) * 4 + z)

    flights = {}
    count = [0]

    def send(key, src, dst, device):
        idx = count[0]
        count[0] += 1
        copy = pltpu.make_async_remote_copy(
            src_ref=src, dst_ref=dst, send_sem=send_sem.at[idx], recv_sem=recv_sem.at[idx],
            device_id=device, device_id_type=MESH,
        )
        copy.start()
        flights[key] = copy

    def arrived(*key):
        flights[key].wait_recv()

    pending = {}

    def fetch(name, src, dst):
        copy = pltpu.make_async_copy(src, dst, in_sem.at[len(pending)])
        copy.start()
        pending[name] = copy

    def tile(j):
        return pl.ds(j * TILE, TILE)

    fetch("p2", p2, p_v.at[1])
    fetch("p3", p3, p_v.at[2])
    fetch("e1", e1, e_v.at[0])
    fetch("e2", e2, e_v.at[1])
    fetch("p1", p1, p_v.at[0])
    fetch("leaf", leaf, leaf_v)
    fetch("rhs0", rhs.at[:, :, tile(0)], rhs_v.at[:, :, tile(0)])
    fetch("c1", c1, c1_v)
    fetch("c2", c2.at[:, pl.ds(pl.multiple_of(x * R, R), R), :], c2_v)
    fetch("c3", c3.at[:, pl.ds(pl.multiple_of((x // 2) * R, R), R), :], c3_v)
    fetch("e3", e3, e_v.at[2])
    fetch("rhs1", rhs.at[:, :, tile(1)], rhs_v.at[:, :, tile(1)])
    fetch("rhs2", rhs.at[:, :, tile(2)], rhs_v.at[:, :, tile(2)])

    barrier = pltpu.get_barrier_semaphore()
    peers = [dev(lax.rem(n + d, 8), w) for d in range(1, 8)]
    peers += [z_dev(d) for d in range(1, 4)] + [x_dev(d) for d in range(1, 4)]
    for peer in peers:
        pl.semaphore_signal(barrier, inc=1, device_id=peer, device_id_type=MESH)

    for name in ("p2", "p3"):
        pending[name].wait()

    def prepare_projection(l, carry):
        at = pl.ds(pl.multiple_of(l * R, R), R)
        re, im = p_v[l, 0].T, p_v[l, 1].T
        for v, value in enumerate((re, -im, re - im)):
            pthi[v, at, :], ptlo[v, at, :] = halves(value)
        return carry

    lax.fori_loop(1, 3, prepare_projection, 0)

    pending["e1"].wait()
    pending["e2"].wait()
    for e, low, mats in ((0, 1, (0, 1)), (1, 2, (2,))):
        lines = pl.ds(low * R, (3 - low) * R)
        t = []
        for v, value in enumerate((e_v[e, 0], e_v[e, 1], e_v[e, 0] + e_v[e, 1])):
            hi, lo = halves(value)
            t.append(dot_nn(pthi[v, lines, :], ptlo[v, lines, :], hi, lo))
        pieces = combine(t)
        for k, m in enumerate(mats):
            for part in range(2):
                g_loc[:, 2 * m + part] = pieces[part][k * R : (k + 1) * R, :].reshape(8, 16, R)
    pl.semaphore_wait(barrier, len(peers))
    for d in range(1, 8):
        to = lax.rem(n + d, 8)
        send(("g", d), g_loc.at[to], g_rs.at[d - 1], dev(to, w))

    def sides(value, flag):
        left, right = value[:, :R], value[:, R:]
        return jnp.where(flag == 0, left, right), jnp.where(flag == 0, right, left)

    def factor_one():
        for d in range(1, 8):
            arrived("g", d)
        total = g_loc[n]
        for d in range(7):
            total = total + g_rs[d]
        for part in range(2):
            z_send[part] = total[4 + part]
        for d in (2, 1, 3):
            send(("gz", d), z_send, z_recv.at[d - 1], z_dev(d))
        pending["c1"].wait()
        both = wide_product(
            jnp.concatenate([total[0], total[2]], axis=0), jnp.concatenate([total[1], total[3]], axis=0), c1_v
        )
        for part in range(2):
            h_mine[part], f_send[part] = sides(both[part], b)
        send(("f",), f_send, f_recv, sibling)

    def factor_two():
        for d in (2, 1, 3):
            arrived("gz", d)
        total = [z_send[part] + z_recv[0, part] + z_recv[1, part] + z_recv[2, part] for part in range(2)]
        pending["c2"].wait()
        both = wide_product(total[0], total[1], c2_v)
        for part in range(2):
            m_mine[part], x_send[part] = sides(both[part], xb)
        send(("m",), x_send, x_recv, x_mate)

    def factor_three():
        arrived("f")
        arrived("m")
        for part in range(2):
            h = h_mine[part] + f_recv[part]
            g_full[n, part] = h[:16]
            g_full[n, 2 + part] = h[16:]
            g_full[n, 4 + part] = m_mine[part] + x_recv[part]
        for d in range(1, 8):
            send(("ag", d), g_full.at[n], g_full.at[n], dev(lax.rem(n + d, 8), w))

    def factor_four():
        for d in range(1, 8):
            arrived("ag", d)
        h = [jnp.concatenate([g_full[:, part].reshape(R, R), g_full[:, 2 + part].reshape(R, R)], axis=0) for part in range(2)]
        store_cat(hcat, h[0], h[1])
        store_cat(mcat, g_full[:, 4].reshape(R, R), g_full[:, 5].reshape(R, R))

    pending["p1"].wait()
    prepare_projection(0, 0)
    pending["leaf"].wait()

    def split_leaf(q, carry):
        at = pl.ds(pl.multiple_of(q * 128, 128), 128)
        re, im = leaf_v[0, at, :], leaf_v[1, at, :]
        for v, value in enumerate((re, im, re + im)):
            lhi[v, at, :], llo[v, at, :] = halves(value)
        return carry

    lax.fori_loop(0, 8, split_leaf, 0)
    def solve(j, first, last):
        def one(l, carry):
            rows = pl.ds(pl.multiple_of(l * LEAF, LEAF), LEAF)
            cols = tile(j)
            b_re, b_im = rhs_v[0, rows, cols], rhs_v[1, rows, cols]
            t = []
            for v, value in enumerate((b_re, b_im, b_re + b_im)):
                hi, lo = halves(value)
                t.append(dot_nn(lhi[v, rows, :], llo[v, rows, :], hi, lo))
            re, im = combine(t)
            rhs_v[0, rows, cols] = re
            rhs_v[1, rows, cols] = im
            for v, value in enumerate((re, im, re + im)):
                yhi[v, rows, :], ylo[v, rows, :] = halves(value)
            return carry

        lax.fori_loop(first, last, one, 0)

    def project(j):
        t = [dot_nn(pthi[v], ptlo[v], yhi[v], ylo[v]) for v in range(3)]
        for part, value in enumerate(combine(t)):
            for l in range(3):
                zt[l, part, j] = value[l * R : (l + 1) * R, :].T.reshape(4, 2, 4, 8, R)
        send(("a", j), zt.at[:, :, j, :, 1 - c], pair_buf.at[j], partner)

    def sum_pair(j):
        arrived("a", j)
        zt[:, :, j, :, c] = zt[:, :, j, :, c] + pair_buf[j]
        for d in (2, 1, 3):
            send(("b", j, d), zt.at[0, :, j, y_at(d), c], rs_buf.at[j, d - 1], y_dev(d))
            send(("zz", j, d), zt.at[pl.ds(1, 2), :, j, :, c, z_at(d)], rzz.at[j, d - 1], z_dev(d))

    def sum_z(j):
        for d in (1, 3, 2):
            arrived("zz", j, d)
        zs[:, :, j] = zt[1:3, :, j, :, c, z] + rzz[j, 0] + rzz[j, 1] + rzz[j, 2]
        for d in (2, 1, 3):
            send(("yy", j, d), zs.at[:, :, j, y_at(d)], ryy.at[j, d - 1], y_dev(d))

    def stage_one(g, j0, nj):
        js = pl.ds(j0, nj)
        for j in range(j0, j0 + nj):
            for d in (1, 3, 2):
                arrived("b", j, d)
            s_buf[:, j] = zt[0, :, j, y, c] + rs_buf[j, 0] + rs_buf[j, 1] + rs_buf[j, 2]
        stk1[b, :, js] = s_buf[:, js]
        send(("sib", g), stk1.at[b, :, js], stk1.at[b, :, js], sibling)
        q = small_product(s_buf[0, js].reshape(nj * 32, R), s_buf[1, js].reshape(nj * 32, R), hcat)
        for part in range(2):
            for k in range(2):
                cut = q[part][:, k * R : (k + 1) * R].reshape(nj, 4, 8, R)
                for q4 in range(4):
                    tz[q4, k, part, js] = cut[:, q4]
        for d in (2, 1, 3):
            send(("rz", g, d), tz.at[z_at(d), :, :, js], rz.at[d - 1, :, :, js], z_dev(d))

    def stage_two(g, j0, nj):
        js = pl.ds(j0, nj)
        arrived("sib", g)
        pairs = [
            jnp.concatenate([stk1[p, part, js].reshape(nj * 32, R) for p in range(2)], axis=1) for part in range(2)
        ]
        k1 = small_product(pairs[0], pairs[1], c1cat)
        for part in range(2):
            corr[0, part, js, y, c] = k1[part].reshape(nj, 4, 8, R)
        block = corr.at[0, :, js, y, c]
        send(("p", g, 0), block, block, partner)
        for d in (2, 1, 3):
            send(("s", g, 0, d), block, block, y_dev(d))
        for d in (1, 3, 2):
            arrived("rz", g, d)
        for j in range(j0, j0 + nj):
            for d in (1, 3, 2):
                arrived("yy", j, d)
            total = zs[:, :, j, y] + ryy[j, 0] + ryy[j, 1] + ryy[j, 2]
            p_buf[:, :, j] = total - tz[z, :, :, j] - rz[0, :, :, j] - rz[1, :, :, j] - rz[2, :, :, j]
        stk2[xb, :, js] = p_buf[0, :, js]
        send(("xm", g), stk2.at[xb, :, js], stk2.at[xb, :, js], x_mate)
        m = small_product(p_buf[0, 0, js].reshape(nj * 8, R), p_buf[0, 1, js].reshape(nj * 8, R), mcat)
        for part in range(2):
            v3[x, part, js] = p_buf[1, part, js] - m[part].reshape(nj, 8, R)
        for d in (2, 1, 3):
            send(("v", g, d), v3.at[x, :, js], v3.at[x, :, js], x_dev(d))

    def stage_three(g, j0, nj):
        js = pl.ds(j0, nj)
        arrived("xm", g)
        pairs = [jnp.concatenate([stk2[p, part, js].reshape(nj * 8, R) for p in range(2)], axis=1) for part in range(2)]
        k2 = small_product(pairs[0], pairs[1], c2cat)
        for part in range(2):
            corr[1, part, js, y, c, z] = k2[part].reshape(nj, 8, R)
        piece = corr.at[1, :, js, y, c, z]
        for d in (2, 1, 3):
            send(("u", g, 1, d), piece, piece, z_dev(d))
        for d in (1, 3, 2):
            arrived("v", g, d)
        pairs = [
            jnp.concatenate(
                [(v3[p, part, js] + v3[p + 1, part, js]).reshape(nj * 8, R) for p in (0, 2)], axis=1
            )
            for part in range(2)
        ]
        k3 = small_product(pairs[0], pairs[1], c3cat)
        for part in range(2):
            corr[2, part, js, y, c, z] = k3[part].reshape(nj, 8, R)
        piece = corr.at[2, :, js, y, c, z]
        for d in (2, 1, 3):
            send(("u", g, 2, d), piece, piece, y_dev(d))

    def forward_y(g, l, j0, nj):
        js = pl.ds(j0, nj)
        for d in (1, 3, 2):
            arrived("s", g, l, d)
            block = corr.at[l, :, js, y_at(4 - d), c]
            send(("f", g, l, d), block, block, partner)

    def stage_four(g, j0, nj):
        js = pl.ds(j0, nj)
        for l, block, to in (
            (1, corr.at[1, :, js, y, c], y_dev),
            (2, corr.at[2, :, js, :, c, z], z_dev),
        ):
            for d in (1, 3, 2):
                arrived("u", g, l, d)
            for d in (2, 1, 3):
                send(("s", g, l, d), block, block, to(d))
            send(("p", g, l), block, block, partner)

    def stage_five(g, j0, nj):
        js = pl.ds(j0, nj)
        forward_y(g, 1, j0, nj)
        for d in (1, 3, 2):
            arrived("s", g, 2, d)
            block = corr.at[2, :, js, :, c, z_at(4 - d)]
            send(("f", g, 2, d), block, block, partner)

    def stage_six(g, j0, nj):
        for l in range(3):
            arrived("p", g, l)
            for d in (1, 3, 2):
                arrived("f", g, l, d)
    def prepare_expansion():
        pending["e3"].wait()

        def one(q, carry):
            at = pl.ds(pl.multiple_of(q * 256, 256), 256)
            for l in range(3):
                re, im = e_v[l, 0, at, :], e_v[l, 1, at, :]
                for v, value in enumerate((re, im, re + im)):
                    ehi[v, at, l * R : (l + 1) * R], elo[v, at, l * R : (l + 1) * R] = halves(value)
            return carry

        lax.fori_loop(0, 4, one, 0)

    def expand(j, start, stop):
        cols = tile(j)
        if start == 0:
            for l in range(3):
                lanes = slice(l * R, (l + 1) * R)
                re, im = corr[l, 0, j].reshape(TILE, R), corr[l, 1, j].reshape(TILE, R)
                for v, value in enumerate((re, im, re + im)):
                    chi[v, :, lanes], clo[v, :, lanes] = halves(value)

        def one(q, carry):
            rows = pl.ds(pl.multiple_of(q * 512, 512), 512)
            re, im = combine([dot_nt(ehi[v, rows, :], elo[v, rows, :], chi[v], clo[v]) for v in range(3)])
            rhs_v[0, rows, cols] = rhs_v[0, rows, cols] - re
            rhs_v[1, rows, cols] = rhs_v[1, rows, cols] - im
            return carry

        lax.fori_loop(start, stop, one, 0)

    first, last = (0, 0, 2), (1, 2, 1)
    pending["rhs0"].wait()
    solve(0, 0, 2)
    project(0)
    factor_one()
    pending["rhs1"].wait()
    solve(1, 0, 1)
    sum_pair(0)
    solve(1, 1, 2)
    factor_two()
    project(1)
    sum_z(0)
    pending["rhs2"].wait()
    solve(2, 0, 1)
    sum_pair(1)
    factor_three()
    solve(2, 1, 2)
    sum_z(1)
    project(2)
    pending["c3"].wait()
    store_cat(c1cat, c1_v[0], c1_v[1])
    store_cat(c2cat, c2_v[0], c2_v[1])
    store_cat(c3cat, c3_v[0], c3_v[1])
    sum_pair(2)
    factor_four()
    stage_one(*first)
    prepare_expansion()
    sum_z(2)
    stage_two(*first)
    stage_one(*last)
    stage_three(*first)
    stage_two(*last)
    forward_y(*first[:1], 0, *first[1:])
    stage_four(*first)
    stage_three(*last)
    stage_five(*first)
    forward_y(*last[:1], 0, *last[1:])
    stage_six(*first)
    stage_four(*last)
    expand(0, 0, 2)
    stage_five(*last)
    expand(1, 0, 1)
    stage_six(*last)
    for l in range(3):
        for part in range(2):
            corr_out[l, part] = corr[l, part, 2].reshape(TILE, R)
    expand(1, 1, 2)

    for copy in flights.values():
        copy.wait_send()


def main_call(rhs, leaf, e1, p1, c1, e2, p2, c2, e3, p3, c3):
    any_spec = pl.BlockSpec(memory_space=pltpu.HBM)
    vm = pltpu.VMEM
    return pl.pallas_call(
        main_kernel,
        out_shape=(
            vm((2, ROWS, NR), F32),
            vm((3, ROWS, 3 * R), BF16),
            vm((3, ROWS, 3 * R), BF16),
            vm((3, 2, TILE, R), F32),
        ),
        in_specs=[any_spec] * 11,
        out_specs=(pl.BlockSpec(memory_space=vm),) * 4,
        scratch_shapes=[
            vm((2, ROWS, LEAF), F32),
            vm((3, 2, ROWS, R), F32),
            vm((3, 2, ROWS, R), F32),
            vm((2, R, 2 * R), F32),
            vm((2, R, 2 * R), F32),
            vm((2, R, 2 * R), F32),
            vm((3, ROWS, LEAF), BF16),
            vm((3, ROWS, LEAF), BF16),
            vm((3, ROWS, TILE), BF16),
            vm((3, ROWS, TILE), BF16),
            vm((3, 3 * R, ROWS), BF16),
            vm((3, 3 * R, ROWS), BF16),
            vm((3, 2, 3, 4, 2, 4, 8, R), F32),
            vm((3, 3, 2, 4, 4, 8, R), F32),
            vm((3, 3, 2, 4, 8, R), F32),
            vm((3, 3, 2, 2, 4, 8, R), F32),
            vm((2, 2, 3, 4, 8, R), F32),
            vm((3, 3, 2, 2, 8, R), F32),
            vm((2, 3, 4, 8, R), F32),
            vm((2, 2, 3, 8, R), F32),
            vm((3, 2, 3, 4, 2, 4, 8, R), F32),
            vm((8, 6, 16, R), F32),
            vm((7, 6, 16, R), F32),
            vm((8, 6, 16, R), F32),
            vm((2, 32, R), F32),
            vm((2, 32, R), F32),
            vm((2, 32, R), F32),
            vm((2, 16, R), F32),
            vm((3, 2, 16, R), F32),
            vm((2, 16, R), F32),
            vm((2, 16, R), F32),
            vm((2, 16, R), F32),
            vm((3, TILE, 3 * R), BF16),
            vm((3, TILE, 3 * R), BF16),
            vm((3, 2 * R, 3 * R), BF16),
            vm((3, R, 3 * R), BF16),
            vm((3, R, 6 * R), BF16),
            vm((3, R, 6 * R), BF16),
            vm((3, R, 6 * R), BF16),
            vm((2, 2, 3, 4, 8, R), F32),
            vm((4, 2, 2, 3, 8, R), F32),
            vm((3, 2, 2, 3, 8, R), F32),
            vm((2, 2, 3, 8, R), F32),
            vm((4, 2, 3, 8, R), F32),
            pltpu.SemaphoreType.DMA((17,)),
            pltpu.SemaphoreType.DMA((NSEM,)),
            pltpu.SemaphoreType.DMA((NSEM,)),
        ],
        compiler_params=pltpu.CompilerParams(
            collective_id=0, has_side_effects=True, vmem_limit_bytes=48 * 1024 * 1024
        ),
        cost_estimate=pl.CostEstimate(flops=14_000_000_000, bytes_accessed=26_000_000, transcendentals=0),
    )(rhs, leaf, e1, p1, c1, e2, p2, c2, e3, p3, c3)


def expand_kernel(y, ehi, elo, corr, out, chi, clo, last, sem):
    done = NR - TILE
    copies = []

    def put(src, dst):
        copy = pltpu.make_async_copy(src, dst, sem.at[len(copies)])
        copy.start()
        copies.append(copy)

    put(y.at[:, :, pl.ds(0, done)], out.at[:, :, pl.ds(0, done)])
    for l in range(3):
        lanes = slice(l * R, (l + 1) * R)
        re, im = corr[l, 0], corr[l, 1]
        for v, value in enumerate((re, im, re + im)):
            chi[v, :, lanes], clo[v, :, lanes] = halves(value)
    cols = pl.ds(done, TILE)
    for q in range(2):
        rows = pl.ds(q * 512, 512)
        re, im = combine([dot_nt(ehi[v, rows, :], elo[v, rows, :], chi[v], clo[v]) for v in range(3)])
        last[0, rows, :] = y[0, rows, cols] - re
        last[1, rows, :] = y[1, rows, cols] - im
        put(last.at[:, rows, :], out.at[:, rows, cols])
    for copy in copies:
        copy.wait()


def expand_call(y, ehi, elo, corr):
    vm = pltpu.VMEM
    return pl.pallas_call(
        expand_kernel,
        out_shape=jax.ShapeDtypeStruct((2, ROWS, NR), F32),
        in_specs=[pl.BlockSpec(memory_space=vm)] * 4,
        out_specs=pl.BlockSpec(memory_space=pltpu.HBM),
        scratch_shapes=[
            vm((3, TILE, 3 * R), BF16),
            vm((3, TILE, 3 * R), BF16),
            vm((2, ROWS, TILE), F32),
            pltpu.SemaphoreType.DMA((3,)),
        ],
        compiler_params=pltpu.CompilerParams(vmem_limit_bytes=20 * 1024 * 1024),
        cost_estimate=pl.CostEstimate(flops=1_800_000_000, bytes_accessed=6_300_000, transcendentals=0),
    )(y, ehi, elo, corr)


def body(rhs, leaf, e1, p1, c1, e2, p2, c2, e3, p3, c3):
    return expand_call(*main_call(rhs, leaf, e1, p1, c1, e2, p2, c2, e3, p3, c3))


def solution(mesh):
    split = P(None, ("wide", "narrow"), None)
    placed = (split, split, split, split, P(None, "wide", None), split, split, P(), split, split, P())
    return jax.shard_map(body, mesh=mesh, in_specs=placed, out_specs=split, check_vma=False)
```

```python
import functools

import jax
import jax.numpy as jnp
from jax import lax
from jax.experimental import pallas as pl
from jax.experimental.pallas import tpu as pltpu
from jax.sharding import PartitionSpec as P

MESH = pl.DeviceIdType.MESH
F32 = jnp.float32
BF16 = jnp.bfloat16
LEAF = 512
R = 128
NR = 768
ROWS = 1024
TILE = 256
NSEM = 120
NT = (((1,), (1,)), ((), ()))


def halves(x):
    hi = x.astype(BF16)
    return hi, (x - hi.astype(F32)).astype(BF16)


def dot_nn(a_hi, a_lo, b_hi, b_lo):
    a = jnp.concatenate([a_hi, a_lo, a_hi], axis=1)
    b = jnp.concatenate([b_hi, b_hi, b_lo], axis=0)
    return jnp.dot(a, b, preferred_element_type=F32)


def dot_nt(a_hi, a_lo, b_hi, b_lo):
    a = jnp.concatenate([a_hi, a_lo, a_hi], axis=1)
    b = jnp.concatenate([b_hi, b_hi, b_lo], axis=1)
    return lax.dot_general(a, b, NT, preferred_element_type=F32)


def combine(t):
    return t[0] - t[1], t[2] - t[0] - t[1]


def small_product(re, im, cat_ref):
    t = []
    for v, x in enumerate((re, im, re + im)):
        hi, lo = halves(x)
        t.append(
            lax.dot_general(
                jnp.concatenate([hi, lo, hi], axis=1),
                cat_ref[v],
                NT,
                preferred_element_type=F32,
            )
        )
    return combine(t)


def store_cat(cat_ref, re, im):
    for v, x in enumerate((re, im, re + im)):
        hi, lo = halves(x)
        cat_ref[v] = jnp.concatenate([hi, hi, lo], axis=1)


def wide_product(re, im, ref):
    c_re, c_im = ref[0], ref[1]
    t = []
    for left, right in ((re, c_re), (im, c_im), (re + im, c_re + c_im)):
        a_hi, a_lo = halves(left)
        b_hi, b_lo = halves(right)
        t.append(dot_nn(a_hi, a_lo, b_hi, b_lo))
    return combine(t)


def main_kernel(
    rhs, leaf, e1, p1, c1, e2, p2, c2, e3, p3, c3,
    rhs_v, ehi, elo, corr_out,
    leaf_v, e_v, p_v, c1_v, c2_v, c3_v,
    lhi, llo, yhi, ylo, pthi, ptlo,
    zt, pair_buf, rs_buf, rzz, zs, ryy, s_buf, p_buf, corr,
    g_loc, g_rs, g_full, h_mine, f_send, f_recv, z_send, z_recv, m_mine, x_send, x_recv,
    chi, clo, hcat, mcat, c1cat, c2cat, c3cat, stk1, tz, rz, stk2, v3,
    in_sem, send_sem, recv_sem,
):
    n = lax.axis_index("narrow")
    w = lax.axis_index("wide")
    y, c = n // 2, lax.rem(n, 2)
    x, z = w // 4, lax.rem(w, 4)
    b, xb = lax.rem(z, 2), lax.rem(x, 2)

    def dev(nn, ww):
        return {"narrow": nn, "wide": ww}

    partner = dev(n + 1 - 2 * c, w)
    sibling = dev(n, w + 1 - 2 * b)
    x_mate = dev(n, w + 4 - 8 * xb)

    def y_at(d):
        return lax.rem(y + d, 4)

    def z_at(d):
        return lax.rem(z + d, 4)

    def y_dev(d):
        return dev(2 * y_at(d) + c, w)

    def z_dev(d):
        return dev(n, x * 4 + z_at(d))

    def x_dev(d):
        return dev(n, lax.rem(x + d, 4) * 4 + z)

    flights = {}
    count = [0]

    def send(key, src, dst, device):
        idx = count[0]
        count[0] += 1
        copy = pltpu.make_async_remote_copy(
            src_ref=src, dst_ref=dst, send_sem=send_sem.at[idx], recv_sem=recv_sem.at[idx],
            device_id=device, device_id_type=MESH,
        )
        copy.start()
        flights[key] = copy

    def arrived(*key):
        flights[key].wait_recv()

    pending = {}

    def fetch(name, src, dst):
        copy = pltpu.make_async_copy(src, dst, in_sem.at[len(pending)])
        copy.start()
        pending[name] = copy

    def tile(j):
        return pl.ds(j * TILE, TILE)

    fetch("p2", p2, p_v.at[1])
    fetch("p3", p3, p_v.at[2])
    fetch("e1", e1, e_v.at[0])
    fetch("e2", e2, e_v.at[1])
    fetch("p1", p1, p_v.at[0])
    fetch("leaf", leaf, leaf_v)
    fetch("rhs0", rhs.at[:, :, tile(0)], rhs_v.at[:, :, tile(0)])
    fetch("c1", c1, c1_v)
    fetch("c2", c2.at[:, pl.ds(pl.multiple_of(x * R, R), R), :], c2_v)
    fetch("c3", c3.at[:, pl.ds(pl.multiple_of((x // 2) * R, R), R), :], c3_v)
    fetch("e3", e3, e_v.at[2])
    fetch("rhs1", rhs.at[:, :, tile(1)], rhs_v.at[:, :, tile(1)])
    fetch("rhs2", rhs.at[:, :, tile(2)], rhs_v.at[:, :, tile(2)])

    barrier = pltpu.get_barrier_semaphore()
    peers = [dev(lax.rem(n + d, 8), w) for d in range(1, 8)]
    peers += [z_dev(d) for d in range(1, 4)] + [x_dev(d) for d in range(1, 4)]
    for peer in peers:
        pl.semaphore_signal(barrier, inc=1, device_id=peer, device_id_type=MESH)

    for name in ("p2", "p3"):
        pending[name].wait()

    def prepare_projection(l, carry):
        at = pl.ds(pl.multiple_of(l * R, R), R)
        re, im = p_v[l, 0].T, p_v[l, 1].T
        for v, value in enumerate((re, -im, re - im)):
            pthi[v, at, :], ptlo[v, at, :] = halves(value)
        return carry

    lax.fori_loop(1, 3, prepare_projection, 0)

    pending["e1"].wait()
    pending["e2"].wait()
    re, im = [jnp.concatenate([e_v[0, part], e_v[1, part]], axis=1) for part in range(2)]
    lines = pl.ds(R, 2 * R)
    t = []
    for v, value in enumerate((re, im, re + im)):
        hi, lo = halves(value)
        t.append(dot_nn(pthi[v, lines, :], ptlo[v, lines, :], hi, lo))
    for part, value in enumerate(combine(t)):
        g_loc[:, part] = value[:R, :R].reshape(8, 16, R)
        g_loc[:, 2 + part] = value[R:, :R].reshape(8, 16, R)
        g_loc[:, 4 + part] = value[R:, R:].reshape(8, 16, R)
    pl.semaphore_wait(barrier, len(peers))
    for d in range(1, 8):
        to = lax.rem(n + d, 8)
        send(("g", d), g_loc.at[to], g_rs.at[d - 1], dev(to, w))

    def sides(value, flag):
        left, right = value[:, :R], value[:, R:]
        return jnp.where(flag == 0, left, right), jnp.where(flag == 0, right, left)

    def factor_one():
        for d in range(1, 8):
            arrived("g", d)
        total = g_loc[n]
        for d in range(7):
            total = total + g_rs[d]
        for part in range(2):
            z_send[part] = total[4 + part]
        for d in (2, 1, 3):
            send(("gz", d), z_send, z_recv.at[d - 1], z_dev(d))
        pending["c1"].wait()
        both = wide_product(
            jnp.concatenate([total[0], total[2]], axis=0), jnp.concatenate([total[1], total[3]], axis=0), c1_v
        )
        for part in range(2):
            h_mine[part], f_send[part] = sides(both[part], b)
        send(("f",), f_send, f_recv, sibling)

    def factor_two():
        for d in (2, 1, 3):
            arrived("gz", d)
        total = [z_send[part] + z_recv[0, part] + z_recv[1, part] + z_recv[2, part] for part in range(2)]
        pending["c2"].wait()
        both = wide_product(total[0], total[1], c2_v)
        for part in range(2):
            m_mine[part], x_send[part] = sides(both[part], xb)
        send(("m",), x_send, x_recv, x_mate)

    def factor_three():
        arrived("f")
        arrived("m")
        for part in range(2):
            h = h_mine[part] + f_recv[part]
            g_full[n, part] = h[:16]
            g_full[n, 2 + part] = h[16:]
            g_full[n, 4 + part] = m_mine[part] + x_recv[part]
        for d in range(1, 8):
            send(("ag", d), g_full.at[n], g_full.at[n], dev(lax.rem(n + d, 8), w))

    def factor_four():
        for d in range(1, 8):
            arrived("ag", d)
        h = [jnp.concatenate([g_full[:, part].reshape(R, R), g_full[:, 2 + part].reshape(R, R)], axis=0) for part in range(2)]
        store_cat(hcat, h[0], h[1])
        store_cat(mcat, g_full[:, 4].reshape(R, R), g_full[:, 5].reshape(R, R))

    pending["p1"].wait()
    prepare_projection(0, 0)
    pending["leaf"].wait()

    def split_leaf(q, carry):
        at = pl.ds(pl.multiple_of(q * 128, 128), 128)
        re, im = leaf_v[0, at, :], leaf_v[1, at, :]
        for v, value in enumerate((re, im, re + im)):
            lhi[v, at, :], llo[v, at, :] = halves(value)
        return carry

    lax.fori_loop(0, 8, split_leaf, 0)
    def solve(j, first, last):
        def one(l, carry):
            rows = pl.ds(pl.multiple_of(l * LEAF, LEAF), LEAF)
            cols = tile(j)
            b_re, b_im = rhs_v[0, rows, cols], rhs_v[1, rows, cols]
            t = []
            for v, value in enumerate((b_re, b_im, b_re + b_im)):
                hi, lo = halves(value)
                t.append(dot_nn(lhi[v, rows, :], llo[v, rows, :], hi, lo))
            re, im = combine(t)
            rhs_v[0, rows, cols] = re
            rhs_v[1, rows, cols] = im
            for v, value in enumerate((re, im, re + im)):
                yhi[v, rows, :], ylo[v, rows, :] = halves(value)
            return carry

        lax.fori_loop(first, last, one, 0)

    def project(j):
        t = [dot_nn(pthi[v], ptlo[v], yhi[v], ylo[v]) for v in range(3)]
        for part, value in enumerate(combine(t)):
            for l in range(3):
                zt[l, part, j] = value[l * R : (l + 1) * R, :].T.reshape(4, 2, 4, 8, R)
        send(("a", j), zt.at[:, :, j, :, 1 - c], pair_buf.at[j], partner)

    def sum_pair(j):
        arrived("a", j)
        zt[:, :, j, :, c] = zt[:, :, j, :, c] + pair_buf[j]
        for d in (2, 1, 3):
            send(("b", j, d), zt.at[0, :, j, y_at(d), c], rs_buf.at[j, d - 1], y_dev(d))
            send(("zz", j, d), zt.at[pl.ds(1, 2), :, j, :, c, z_at(d)], rzz.at[j, d - 1], z_dev(d))

    def sum_z(j):
        for d in (1, 3, 2):
            arrived("zz", j, d)
        zs[:, :, j] = zt[1:3, :, j, :, c, z] + rzz[j, 0] + rzz[j, 1] + rzz[j, 2]
        for d in (2, 1, 3):
            send(("yy", j, d), zs.at[:, :, j, y_at(d)], ryy.at[j, d - 1], y_dev(d))

    def stage_one(g, j0, nj):
        js = pl.ds(j0, nj)
        for j in range(j0, j0 + nj):
            for d in (1, 3, 2):
                arrived("b", j, d)
            s_buf[:, j] = zt[0, :, j, y, c] + rs_buf[j, 0] + rs_buf[j, 1] + rs_buf[j, 2]
        stk1[b, :, js] = s_buf[:, js]
        send(("sib", g), stk1.at[b, :, js], stk1.at[b, :, js], sibling)
        q = small_product(s_buf[0, js].reshape(nj * 32, R), s_buf[1, js].reshape(nj * 32, R), hcat)
        for part in range(2):
            for k in range(2):
                cut = q[part][:, k * R : (k + 1) * R].reshape(nj, 4, 8, R)
                for q4 in range(4):
                    tz[q4, k, part, js] = cut[:, q4]
        for d in (2, 1, 3):
            send(("rz", g, d), tz.at[z_at(d), :, :, js], rz.at[d - 1, :, :, js], z_dev(d))

    def stage_two(g, j0, nj):
        js = pl.ds(j0, nj)
        arrived("sib", g)
        pairs = [
            jnp.concatenate([stk1[p, part, js].reshape(nj * 32, R) for p in range(2)], axis=1) for part in range(2)
        ]
        k1 = small_product(pairs[0], pairs[1], c1cat)
        for part in range(2):
            corr[0, part, js, y, c] = k1[part].reshape(nj, 4, 8, R)
        block = corr.at[0, :, js, y, c]
        send(("p", g, 0), block, block, partner)
        for d in (2, 1, 3):
            send(("s", g, 0, d), block, block, y_dev(d))
        for d in (1, 3, 2):
            arrived("rz", g, d)
        for j in range(j0, j0 + nj):
            for d in (1, 3, 2):
                arrived("yy", j, d)
            total = zs[:, :, j, y] + ryy[j, 0] + ryy[j, 1] + ryy[j, 2]
            p_buf[:, :, j] = total - tz[z, :, :, j] - rz[0, :, :, j] - rz[1, :, :, j] - rz[2, :, :, j]
        stk2[xb, :, js] = p_buf[0, :, js]
        send(("xm", g), stk2.at[xb, :, js], stk2.at[xb, :, js], x_mate)
        m = small_product(p_buf[0, 0, js].reshape(nj * 8, R), p_buf[0, 1, js].reshape(nj * 8, R), mcat)
        for part in range(2):
            v3[x, part, js] = p_buf[1, part, js] - m[part].reshape(nj, 8, R)
        for d in (2, 1, 3):
            send(("v", g, d), v3.at[x, :, js], v3.at[x, :, js], x_dev(d))

    def stage_three(g, j0, nj):
        js = pl.ds(j0, nj)
        arrived("xm", g)
        pairs = [jnp.concatenate([stk2[p, part, js].reshape(nj * 8, R) for p in range(2)], axis=1) for part in range(2)]
        k2 = small_product(pairs[0], pairs[1], c2cat)
        for part in range(2):
            corr[1, part, js, y, c, z] = k2[part].reshape(nj, 8, R)
        piece = corr.at[1, :, js, y, c, z]
        for d in (2, 1, 3):
            send(("u", g, 1, d), piece, piece, z_dev(d))
        for d in (1, 3, 2):
            arrived("v", g, d)
        pairs = [
            jnp.concatenate(
                [(v3[p, part, js] + v3[p + 1, part, js]).reshape(nj * 8, R) for p in (0, 2)], axis=1
            )
            for part in range(2)
        ]
        k3 = small_product(pairs[0], pairs[1], c3cat)
        for part in range(2):
            corr[2, part, js, y, c, z] = k3[part].reshape(nj, 8, R)
        piece = corr.at[2, :, js, y, c, z]
        for d in (2, 1, 3):
            send(("u", g, 2, d), piece, piece, y_dev(d))

    def forward_y(g, l, j0, nj):
        js = pl.ds(j0, nj)
        for d in (1, 3, 2):
            arrived("s", g, l, d)
            block = corr.at[l, :, js, y_at(4 - d), c]
            send(("f", g, l, d), block, block, partner)

    def stage_four(g, j0, nj):
        js = pl.ds(j0, nj)
        for l, block, to in (
            (1, corr.at[1, :, js, y, c], y_dev),
            (2, corr.at[2, :, js, :, c, z], z_dev),
        ):
            for d in (1, 3, 2):
                arrived("u", g, l, d)
            for d in (2, 1, 3):
                send(("s", g, l, d), block, block, to(d))
            send(("p", g, l), block, block, partner)

    def stage_five(g, j0, nj):
        js = pl.ds(j0, nj)
        forward_y(g, 1, j0, nj)
        for d in (1, 3, 2):
            arrived("s", g, 2, d)
            block = corr.at[2, :, js, :, c, z_at(4 - d)]
            send(("f", g, 2, d), block, block, partner)

    def stage_six(g, j0, nj):
        for l in range(3):
            arrived("p", g, l)
            for d in (1, 3, 2):
                arrived("f", g, l, d)
    def prepare_expansion():
        pending["e3"].wait()

        def one(q, carry):
            at = pl.ds(pl.multiple_of(q * 256, 256), 256)
            for l in range(3):
                re, im = e_v[l, 0, at, :], e_v[l, 1, at, :]
                for v, value in enumerate((re, im, re + im)):
                    ehi[v, at, l * R : (l + 1) * R], elo[v, at, l * R : (l + 1) * R] = halves(value)
            return carry

        lax.fori_loop(0, 4, one, 0)

    def expand(j, start, stop):
        cols = tile(j)
        if start == 0:
            for l in range(3):
                lanes = slice(l * R, (l + 1) * R)
                re, im = corr[l, 0, j].reshape(TILE, R), corr[l, 1, j].reshape(TILE, R)
                for v, value in enumerate((re, im, re + im)):
                    chi[v, :, lanes], clo[v, :, lanes] = halves(value)

        def one(q, carry):
            rows = pl.ds(pl.multiple_of(q * 512, 512), 512)
            re, im = combine([dot_nt(ehi[v, rows, :], elo[v, rows, :], chi[v], clo[v]) for v in range(3)])
            rhs_v[0, rows, cols] = rhs_v[0, rows, cols] - re
            rhs_v[1, rows, cols] = rhs_v[1, rows, cols] - im
            return carry

        lax.fori_loop(start, stop, one, 0)

    first, last = (0, 0, 2), (1, 2, 1)
    pending["rhs0"].wait()
    solve(0, 0, 2)
    factor_one()
    project(0)
    pending["rhs1"].wait()
    solve(1, 0, 1)
    sum_pair(0)
    factor_two()
    solve(1, 1, 2)
    project(1)
    sum_z(0)
    factor_three()
    pending["rhs2"].wait()
    solve(2, 0, 1)
    sum_pair(1)
    solve(2, 1, 2)
    sum_z(1)
    project(2)
    factor_four()
    stage_one(*first)
    sum_pair(2)
    pending["c3"].wait()
    store_cat(c1cat, c1_v[0], c1_v[1])
    store_cat(c2cat, c2_v[0], c2_v[1])
    store_cat(c3cat, c3_v[0], c3_v[1])
    prepare_expansion()
    stage_two(*first)
    stage_one(*last)
    sum_z(2)
    stage_three(*first)
    stage_two(*last)
    stage_four(*first)
    forward_y(*first[:1], 0, *first[1:])
    stage_three(*last)
    stage_five(*first)
    forward_y(*last[:1], 0, *last[1:])
    stage_four(*last)
    stage_six(*first)
    expand(0, 0, 2)
    expand(1, 0, 1)
    stage_five(*last)
    expand(1, 1, 2)
    stage_six(*last)
    for l in range(3):
        for part in range(2):
            corr_out[l, part] = corr[l, part, 2].reshape(TILE, R)

    for copy in flights.values():
        copy.wait_send()


def main_call(rhs, leaf, e1, p1, c1, e2, p2, c2, e3, p3, c3):
    any_spec = pl.BlockSpec(memory_space=pltpu.HBM)
    vm = pltpu.VMEM
    return pl.pallas_call(
        main_kernel,
        out_shape=(
            vm((2, ROWS, NR), F32),
            vm((3, ROWS, 3 * R), BF16),
            vm((3, ROWS, 3 * R), BF16),
            vm((3, 2, TILE, R), F32),
        ),
        in_specs=[any_spec] * 11,
        out_specs=(pl.BlockSpec(memory_space=vm),) * 4,
        scratch_shapes=[
            vm((2, ROWS, LEAF), F32),
            vm((3, 2, ROWS, R), F32),
            vm((3, 2, ROWS, R), F32),
            vm((2, R, 2 * R), F32),
            vm((2, R, 2 * R), F32),
            vm((2, R, 2 * R), F32),
            vm((3, ROWS, LEAF), BF16),
            vm((3, ROWS, LEAF), BF16),
            vm((3, ROWS, TILE), BF16),
            vm((3, ROWS, TILE), BF16),
            vm((3, 3 * R, ROWS), BF16),
            vm((3, 3 * R, ROWS), BF16),
            vm((3, 2, 3, 4, 2, 4, 8, R), F32),
            vm((3, 3, 2, 4, 4, 8, R), F32),
            vm((3, 3, 2, 4, 8, R), F32),
            vm((3, 3, 2, 2, 4, 8, R), F32),
            vm((2, 2, 3, 4, 8, R), F32),
            vm((3, 3, 2, 2, 8, R), F32),
            vm((2, 3, 4, 8, R), F32),
            vm((2, 2, 3, 8, R), F32),
            vm((3, 2, 3, 4, 2, 4, 8, R), F32),
            vm((8, 6, 16, R), F32),
            vm((7, 6, 16, R), F32),
            vm((8, 6, 16, R), F32),
            vm((2, 32, R), F32),
            vm((2, 32, R), F32),
            vm((2, 32, R), F32),
            vm((2, 16, R), F32),
            vm((3, 2, 16, R), F32),
            vm((2, 16, R), F32),
            vm((2, 16, R), F32),
            vm((2, 16, R), F32),
            vm((3, TILE, 3 * R), BF16),
            vm((3, TILE, 3 * R), BF16),
            vm((3, 2 * R, 3 * R), BF16),
            vm((3, R, 3 * R), BF16),
            vm((3, R, 6 * R), BF16),
            vm((3, R, 6 * R), BF16),
            vm((3, R, 6 * R), BF16),
            vm((2, 2, 3, 4, 8, R), F32),
            vm((4, 2, 2, 3, 8, R), F32),
            vm((3, 2, 2, 3, 8, R), F32),
            vm((2, 2, 3, 8, R), F32),
            vm((4, 2, 3, 8, R), F32),
            pltpu.SemaphoreType.DMA((17,)),
            pltpu.SemaphoreType.DMA((NSEM,)),
            pltpu.SemaphoreType.DMA((NSEM,)),
        ],
        compiler_params=pltpu.CompilerParams(
            collective_id=0, has_side_effects=True, vmem_limit_bytes=48 * 1024 * 1024
        ),
        cost_estimate=pl.CostEstimate(flops=14_000_000_000, bytes_accessed=26_000_000, transcendentals=0),
    )(rhs, leaf, e1, p1, c1, e2, p2, c2, e3, p3, c3)


def expand_kernel(y, ehi, elo, corr, out, chi, clo, last, sem):
    done = NR - TILE
    copies = []

    def put(src, dst):
        copy = pltpu.make_async_copy(src, dst, sem.at[len(copies)])
        copy.start()
        copies.append(copy)

    put(y.at[:, :, pl.ds(0, done)], out.at[:, :, pl.ds(0, done)])
    for l in range(3):
        lanes = slice(l * R, (l + 1) * R)
        re, im = corr[l, 0], corr[l, 1]
        for v, value in enumerate((re, im, re + im)):
            chi[v, :, lanes], clo[v, :, lanes] = halves(value)
    cols = pl.ds(done, TILE)
    for q in range(2):
        rows = pl.ds(q * 512, 512)
        re, im = combine([dot_nt(ehi[v, rows, :], elo[v, rows, :], chi[v], clo[v]) for v in range(3)])
        last[0, rows, :] = y[0, rows, cols] - re
        last[1, rows, :] = y[1, rows, cols] - im
        put(last.at[:, rows, :], out.at[:, rows, cols])
    for copy in copies:
        copy.wait()


def expand_call(y, ehi, elo, corr):
    vm = pltpu.VMEM
    return pl.pallas_call(
        expand_kernel,
        out_shape=jax.ShapeDtypeStruct((2, ROWS, NR), F32),
        in_specs=[pl.BlockSpec(memory_space=vm)] * 4,
        out_specs=pl.BlockSpec(memory_space=pltpu.HBM),
        scratch_shapes=[
            vm((3, TILE, 3 * R), BF16),
            vm((3, TILE, 3 * R), BF16),
            vm((2, ROWS, TILE), F32),
            pltpu.SemaphoreType.DMA((3,)),
        ],
        compiler_params=pltpu.CompilerParams(vmem_limit_bytes=20 * 1024 * 1024),
        cost_estimate=pl.CostEstimate(flops=1_800_000_000, bytes_accessed=6_300_000, transcendentals=0),
    )(y, ehi, elo, corr)


def body(rhs, leaf, e1, p1, c1, e2, p2, c2, e3, p3, c3):
    return expand_call(*main_call(rhs, leaf, e1, p1, c1, e2, p2, c2, e3, p3, c3))


def solution(mesh):
    split = P(None, ("wide", "narrow"), None)
    placed = (split, split, split, split, P(None, "wide", None), split, split, P(), split, split, P())
    return jax.shard_map(body, mesh=mesh, in_specs=placed, out_specs=split, check_vma=False)
```

```python
import functools

import jax
import jax.numpy as jnp
from jax import lax
from jax.experimental import pallas as pl
from jax.experimental.pallas import tpu as pltpu
from jax.sharding import PartitionSpec as P

MESH = pl.DeviceIdType.MESH
F32 = jnp.float32
BF16 = jnp.bfloat16
LEAF = 512
R = 128
NR = 768
ROWS = 1024
TILE = 256
NSEM = 120
NT = (((1,), (1,)), ((), ()))


def halves(x):
    hi = x.astype(BF16)
    return hi, (x - hi.astype(F32)).astype(BF16)


def dot_nn(a_hi, a_lo, b_hi, b_lo):
    a = jnp.concatenate([a_hi, a_lo, a_hi], axis=1)
    b = jnp.concatenate([b_hi, b_hi, b_lo], axis=0)
    return jnp.dot(a, b, preferred_element_type=F32)


def dot_nt(a_hi, a_lo, b_hi, b_lo):
    a = jnp.concatenate([a_hi, a_lo, a_hi], axis=1)
    b = jnp.concatenate([b_hi, b_hi, b_lo], axis=1)
    return lax.dot_general(a, b, NT, preferred_element_type=F32)


def combine(t):
    return t[0] - t[1], t[2] - t[0] - t[1]


def small_product(re, im, cat_ref):
    t = []
    for v, x in enumerate((re, im, re + im)):
        hi, lo = halves(x)
        t.append(
            lax.dot_general(
                jnp.concatenate([hi, lo, hi], axis=1),
                cat_ref[v],
                NT,
                preferred_element_type=F32,
            )
        )
    return combine(t)


def store_cat(cat_ref, re, im):
    for v, x in enumerate((re, im, re + im)):
        hi, lo = halves(x)
        cat_ref[v] = jnp.concatenate([hi, hi, lo], axis=1)


def wide_product(re, im, ref):
    c_re, c_im = ref[0], ref[1]
    t = []
    for left, right in ((re, c_re), (im, c_im), (re + im, c_re + c_im)):
        a_hi, a_lo = halves(left)
        b_hi, b_lo = halves(right)
        t.append(dot_nn(a_hi, a_lo, b_hi, b_lo))
    return combine(t)


def main_kernel(
    rhs, leaf, e1, p1, c1, e2, p2, c2, e3, p3, c3,
    rhs_v, ehi, elo, corr_out,
    leaf_v, e_v, p_v, c1_v, c2_v, c3_v,
    lhi, llo, yhi, ylo, pthi, ptlo,
    zt, pair_buf, rs_buf, rzz, zs, ryy, s_buf, p_buf, corr,
    g_loc, g_rs, g_full, h_mine, f_send, f_recv, z_send, z_recv, m_mine, x_send, x_recv,
    chi, clo, hcat, mcat, c1cat, c2cat, c3cat, stk1, tz, rz, stk2, v3,
    in_sem, send_sem, recv_sem,
):
    n = lax.axis_index("narrow")
    w = lax.axis_index("wide")
    y, c = n // 2, lax.rem(n, 2)
    x, z = w // 4, lax.rem(w, 4)
    b, xb = lax.rem(z, 2), lax.rem(x, 2)

    def dev(nn, ww):
        return {"narrow": nn, "wide": ww}

    partner = dev(n + 1 - 2 * c, w)
    sibling = dev(n, w + 1 - 2 * b)
    x_mate = dev(n, w + 4 - 8 * xb)

    def y_at(d):
        return lax.rem(y + d, 4)

    def z_at(d):
        return lax.rem(z + d, 4)

    def y_dev(d):
        return dev(2 * y_at(d) + c, w)

    def z_dev(d):
        return dev(n, x * 4 + z_at(d))

    def x_dev(d):
        return dev(n, lax.rem(x + d, 4) * 4 + z)

    flights = {}
    count = [0]

    def send(key, src, dst, device):
        idx = count[0]
        count[0] += 1
        copy = pltpu.make_async_remote_copy(
            src_ref=src, dst_ref=dst, send_sem=send_sem.at[idx], recv_sem=recv_sem.at[idx],
            device_id=device, device_id_type=MESH,
        )
        copy.start()
        flights[key] = copy

    def arrived(*key):
        flights[key].wait_recv()

    barrier = pltpu.get_barrier_semaphore()
    peers = [dev(lax.rem(n + d, 8), w) for d in range(1, 8)]
    peers += [z_dev(d) for d in range(1, 4)] + [x_dev(d) for d in range(1, 4)]
    for peer in peers:
        pl.semaphore_signal(barrier, inc=1, device_id=peer, device_id_type=MESH)

    pending = {}

    def fetch(name, src, dst):
        copy = pltpu.make_async_copy(src, dst, in_sem.at[len(pending)])
        copy.start()
        pending[name] = copy

    def tile(j):
        return pl.ds(j * TILE, TILE)


    fetch("p2", p2, p_v.at[1])
    fetch("p3", p3, p_v.at[2])
    fetch("e1", e1, e_v.at[0])
    fetch("e2", e2, e_v.at[1])
    for name in ("p2", "p3"):
        pending[name].wait()
    fetch("p1", p1, p_v.at[0])
    fetch("leaf", leaf, leaf_v)

    def prepare_projection(l, carry):
        at = pl.ds(pl.multiple_of(l * R, R), R)
        re, im = p_v[l, 0].T, p_v[l, 1].T
        for v, value in enumerate((re, -im, re - im)):
            pthi[v, at, :], ptlo[v, at, :] = halves(value)
        return carry

    lax.fori_loop(1, 3, prepare_projection, 0)

    pending["e1"].wait()
    pending["e2"].wait()
    fetch("rhs0", rhs.at[:, :, tile(0)], rhs_v.at[:, :, tile(0)])
    fetch("c1", c1, c1_v)
    fetch("c2", c2.at[:, pl.ds(pl.multiple_of(x * R, R), R), :], c2_v)
    fetch("rhs1", rhs.at[:, :, tile(1)], rhs_v.at[:, :, tile(1)])
    re, im = [jnp.concatenate([e_v[0, part], e_v[1, part]], axis=1) for part in range(2)]
    lines = pl.ds(R, 2 * R)
    t = []
    for v, value in enumerate((re, im, re + im)):
        hi, lo = halves(value)
        t.append(dot_nn(pthi[v, lines, :], ptlo[v, lines, :], hi, lo))
    for part, value in enumerate(combine(t)):
        g_loc[:, part] = value[:R, :R].reshape(8, 16, R)
        g_loc[:, 2 + part] = value[R:, :R].reshape(8, 16, R)
        g_loc[:, 4 + part] = value[R:, R:].reshape(8, 16, R)
    pl.semaphore_wait(barrier, len(peers))
    for d in range(1, 8):
        to = lax.rem(n + d, 8)
        send(("g", d), g_loc.at[to], g_rs.at[d - 1], dev(to, w))

    def sides(value, flag):
        left, right = value[:, :R], value[:, R:]
        return jnp.where(flag == 0, left, right), jnp.where(flag == 0, right, left)

    def factor_one():
        for d in range(1, 8):
            arrived("g", d)
        total = g_loc[n]
        for d in range(7):
            total = total + g_rs[d]
        for part in range(2):
            z_send[part] = total[4 + part]
        for d in (2, 1, 3):
            send(("gz", d), z_send, z_recv.at[d - 1], z_dev(d))
        pending["c1"].wait()
        both = wide_product(
            jnp.concatenate([total[0], total[2]], axis=0), jnp.concatenate([total[1], total[3]], axis=0), c1_v
        )
        for part in range(2):
            h_mine[part], f_send[part] = sides(both[part], b)
        send(("f",), f_send, f_recv, sibling)

    def factor_two():
        for d in (2, 1, 3):
            arrived("gz", d)
        total = [z_send[part] + z_recv[0, part] + z_recv[1, part] + z_recv[2, part] for part in range(2)]
        pending["c2"].wait()
        both = wide_product(total[0], total[1], c2_v)
        for part in range(2):
            m_mine[part], x_send[part] = sides(both[part], xb)
        send(("m",), x_send, x_recv, x_mate)

    def factor_three():
        arrived("f")
        arrived("m")
        for part in range(2):
            h = h_mine[part] + f_recv[part]
            g_full[n, part] = h[:16]
            g_full[n, 2 + part] = h[16:]
            g_full[n, 4 + part] = m_mine[part] + x_recv[part]
        for d in range(1, 8):
            send(("ag", d), g_full.at[n], g_full.at[n], dev(lax.rem(n + d, 8), w))

    def factor_four():
        for d in range(1, 8):
            arrived("ag", d)
        h = [jnp.concatenate([g_full[:, part].reshape(R, R), g_full[:, 2 + part].reshape(R, R)], axis=0) for part in range(2)]
        store_cat(hcat, h[0], h[1])
        store_cat(mcat, g_full[:, 4].reshape(R, R), g_full[:, 5].reshape(R, R))

    pending["p1"].wait()
    prepare_projection(0, 0)
    fetch("rhs2", rhs.at[:, :, tile(2)], rhs_v.at[:, :, tile(2)])
    fetch("c3", c3.at[:, pl.ds(pl.multiple_of((x // 2) * R, R), R), :], c3_v)
    fetch("e3", e3, e_v.at[2])
    pending["leaf"].wait()

    def split_leaf(q, carry):
        at = pl.ds(pl.multiple_of(q * 128, 128), 128)
        re, im = leaf_v[0, at, :], leaf_v[1, at, :]
        for v, value in enumerate((re, im, re + im)):
            lhi[v, at, :], llo[v, at, :] = halves(value)
        return carry

    lax.fori_loop(0, 8, split_leaf, 0)
    def solve(j, first, last):
        def one(l, carry):
            rows = pl.ds(pl.multiple_of(l * LEAF, LEAF), LEAF)
            cols = tile(j)
            b_re, b_im = rhs_v[0, rows, cols], rhs_v[1, rows, cols]
            t = []
            for v, value in enumerate((b_re, b_im, b_re + b_im)):
                hi, lo = halves(value)
                t.append(dot_nn(lhi[v, rows, :], llo[v, rows, :], hi, lo))
            re, im = combine(t)
            rhs_v[0, rows, cols] = re
            rhs_v[1, rows, cols] = im
            for v, value in enumerate((re, im, re + im)):
                yhi[v, rows, :], ylo[v, rows, :] = halves(value)
            return carry

        lax.fori_loop(first, last, one, 0)

    def project(j):
        t = [dot_nn(pthi[v], ptlo[v], yhi[v], ylo[v]) for v in range(3)]
        for part, value in enumerate(combine(t)):
            for l in range(3):
                zt[l, part, j] = value[l * R : (l + 1) * R, :].T.reshape(4, 2, 4, 8, R)
        send(("a", j), zt.at[:, :, j, :, 1 - c], pair_buf.at[j], partner)

    def sum_pair(j):
        arrived("a", j)
        zt[:, :, j, :, c] = zt[:, :, j, :, c] + pair_buf[j]
        for d in (2, 1, 3):
            send(("b", j, d), zt.at[0, :, j, y_at(d), c], rs_buf.at[j, d - 1], y_dev(d))
            send(("zz", j, d), zt.at[pl.ds(1, 2), :, j, :, c, z_at(d)], rzz.at[j, d - 1], z_dev(d))

    def sum_z(j):
        for d in (1, 3, 2):
            arrived("zz", j, d)
        zs[:, :, j] = zt[1:3, :, j, :, c, z] + rzz[j, 0] + rzz[j, 1] + rzz[j, 2]
        for d in (2, 1, 3):
            send(("yy", j, d), zs.at[:, :, j, y_at(d)], ryy.at[j, d - 1], y_dev(d))

    def stage_one(g, j0, nj):
        js = pl.ds(j0, nj)
        for j in range(j0, j0 + nj):
            for d in (1, 3, 2):
                arrived("b", j, d)
            s_buf[:, j] = zt[0, :, j, y, c] + rs_buf[j, 0] + rs_buf[j, 1] + rs_buf[j, 2]
        stk1[b, :, js] = s_buf[:, js]
        send(("sib", g), stk1.at[b, :, js], stk1.at[b, :, js], sibling)
        q = small_product(s_buf[0, js].reshape(nj * 32, R), s_buf[1, js].reshape(nj * 32, R), hcat)
        for part in range(2):
            for k in range(2):
                cut = q[part][:, k * R : (k + 1) * R].reshape(nj, 4, 8, R)
                for q4 in range(4):
                    tz[q4, k, part, js] = cut[:, q4]
        for d in (2, 1, 3):
            send(("rz", g, d), tz.at[z_at(d), :, :, js], rz.at[d - 1, :, :, js], z_dev(d))

    def stage_two(g, j0, nj):
        js = pl.ds(j0, nj)
        arrived("sib", g)
        pairs = [
            jnp.concatenate([stk1[p, part, js].reshape(nj * 32, R) for p in range(2)], axis=1) for part in range(2)
        ]
        k1 = small_product(pairs[0], pairs[1], c1cat)
        for part in range(2):
            corr[0, part, js, y, c] = k1[part].reshape(nj, 4, 8, R)
        block = corr.at[0, :, js, y, c]
        send(("p", g, 0), block, block, partner)
        for d in (2, 1, 3):
            send(("s", g, 0, d), block, block, y_dev(d))
        for d in (1, 3, 2):
            arrived("rz", g, d)
        for j in range(j0, j0 + nj):
            for d in (1, 3, 2):
                arrived("yy", j, d)
            total = zs[:, :, j, y] + ryy[j, 0] + ryy[j, 1] + ryy[j, 2]
            p_buf[:, :, j] = total - tz[z, :, :, j] - rz[0, :, :, j] - rz[1, :, :, j] - rz[2, :, :, j]
        stk2[xb, :, js] = p_buf[0, :, js]
        send(("xm", g), stk2.at[xb, :, js], stk2.at[xb, :, js], x_mate)
        m = small_product(p_buf[0, 0, js].reshape(nj * 8, R), p_buf[0, 1, js].reshape(nj * 8, R), mcat)
        for part in range(2):
            v3[x, part, js] = p_buf[1, part, js] - m[part].reshape(nj, 8, R)
        for d in (2, 1, 3):
            send(("v", g, d), v3.at[x, :, js], v3.at[x, :, js], x_dev(d))

    def stage_three(g, j0, nj):
        js = pl.ds(j0, nj)
        arrived("xm", g)
        pairs = [jnp.concatenate([stk2[p, part, js].reshape(nj * 8, R) for p in range(2)], axis=1) for part in range(2)]
        k2 = small_product(pairs[0], pairs[1], c2cat)
        for part in range(2):
            corr[1, part, js, y, c, z] = k2[part].reshape(nj, 8, R)
        piece = corr.at[1, :, js, y, c, z]
        for d in (2, 1, 3):
            send(("u", g, 1, d), piece, piece, z_dev(d))
        for d in (1, 3, 2):
            arrived("v", g, d)
        pairs = [
            jnp.concatenate(
                [(v3[p, part, js] + v3[p + 1, part, js]).reshape(nj * 8, R) for p in (0, 2)], axis=1
            )
            for part in range(2)
        ]
        k3 = small_product(pairs[0], pairs[1], c3cat)
        for part in range(2):
            corr[2, part, js, y, c, z] = k3[part].reshape(nj, 8, R)
        piece = corr.at[2, :, js, y, c, z]
        for d in (2, 1, 3):
            send(("u", g, 2, d), piece, piece, y_dev(d))

    def forward_y(g, l, j0, nj):
        js = pl.ds(j0, nj)
        for d in (1, 3, 2):
            arrived("s", g, l, d)
            block = corr.at[l, :, js, y_at(4 - d), c]
            send(("f", g, l, d), block, block, partner)

    def stage_four(g, j0, nj):
        js = pl.ds(j0, nj)
        for l, block, to in (
            (1, corr.at[1, :, js, y, c], y_dev),
            (2, corr.at[2, :, js, :, c, z], z_dev),
        ):
            for d in (1, 3, 2):
                arrived("u", g, l, d)
            for d in (2, 1, 3):
                send(("s", g, l, d), block, block, to(d))
            send(("p", g, l), block, block, partner)

    def stage_five(g, j0, nj):
        js = pl.ds(j0, nj)
        forward_y(g, 1, j0, nj)
        for d in (1, 3, 2):
            arrived("s", g, 2, d)
            block = corr.at[2, :, js, :, c, z_at(4 - d)]
            send(("f", g, 2, d), block, block, partner)

    def stage_six(g, j0, nj):
        for l in range(3):
            arrived("p", g, l)
            for d in (1, 3, 2):
                arrived("f", g, l, d)
    def prepare_expansion():
        pending["e3"].wait()

        def one(q, carry):
            at = pl.ds(pl.multiple_of(q * 256, 256), 256)
            for l in range(3):
                re, im = e_v[l, 0, at, :], e_v[l, 1, at, :]
                for v, value in enumerate((re, im, re + im)):
                    ehi[v, at, l * R : (l + 1) * R], elo[v, at, l * R : (l + 1) * R] = halves(value)
            return carry

        lax.fori_loop(0, 4, one, 0)

    def expand(j, start, stop):
        cols = tile(j)
        if start == 0:
            for l in range(3):
                lanes = slice(l * R, (l + 1) * R)
                re, im = corr[l, 0, j].reshape(TILE, R), corr[l, 1, j].reshape(TILE, R)
                for v, value in enumerate((re, im, re + im)):
                    chi[v, :, lanes], clo[v, :, lanes] = halves(value)

        def one(q, carry):
            rows = pl.ds(pl.multiple_of(q * 512, 512), 512)
            re, im = combine([dot_nt(ehi[v, rows, :], elo[v, rows, :], chi[v], clo[v]) for v in range(3)])
            rhs_v[0, rows, cols] = rhs_v[0, rows, cols] - re
            rhs_v[1, rows, cols] = rhs_v[1, rows, cols] - im
            return carry

        lax.fori_loop(start, stop, one, 0)

    first, last = (0, 0, 2), (1, 2, 1)
    pending["rhs0"].wait()
    solve(0, 0, 2)
    project(0)
    factor_one()
    pending["rhs1"].wait()
    solve(1, 0, 1)
    sum_pair(0)
    solve(1, 1, 2)
    factor_two()
    project(1)
    sum_z(0)
    pending["rhs2"].wait()
    solve(2, 0, 1)
    sum_pair(1)
    factor_three()
    solve(2, 1, 2)
    sum_z(1)
    project(2)
    factor_four()
    stage_one(*first)
    sum_pair(2)
    pending["c3"].wait()
    store_cat(c1cat, c1_v[0], c1_v[1])
    store_cat(c2cat, c2_v[0], c2_v[1])
    store_cat(c3cat, c3_v[0], c3_v[1])
    prepare_expansion()
    stage_two(*first)
    stage_one(*last)
    sum_z(2)
    stage_three(*first)
    stage_two(*last)
    stage_four(*first)
    forward_y(*first[:1], 0, *first[1:])
    stage_three(*last)
    stage_five(*first)
    forward_y(*last[:1], 0, *last[1:])
    stage_four(*last)
    stage_six(*first)
    expand(0, 0, 2)
    expand(1, 0, 1)
    stage_five(*last)
    expand(1, 1, 2)
    stage_six(*last)
    for l in range(3):
        for part in range(2):
            corr_out[l, part] = corr[l, part, 2].reshape(TILE, R)

    for copy in flights.values():
        copy.wait_send()


def main_call(rhs, leaf, e1, p1, c1, e2, p2, c2, e3, p3, c3):
    any_spec = pl.BlockSpec(memory_space=pltpu.HBM)
    vm = pltpu.VMEM
    return pl.pallas_call(
        main_kernel,
        out_shape=(
            vm((2, ROWS, NR), F32),
            vm((3, ROWS, 3 * R), BF16),
            vm((3, ROWS, 3 * R), BF16),
            vm((3, 2, TILE, R), F32),
        ),
        in_specs=[any_spec] * 11,
        out_specs=(pl.BlockSpec(memory_space=vm),) * 4,
        scratch_shapes=[
            vm((2, ROWS, LEAF), F32),
            vm((3, 2, ROWS, R), F32),
            vm((3, 2, ROWS, R), F32),
            vm((2, R, 2 * R), F32),
            vm((2, R, 2 * R), F32),
            vm((2, R, 2 * R), F32),
            vm((3, ROWS, LEAF), BF16),
            vm((3, ROWS, LEAF), BF16),
            vm((3, ROWS, TILE), BF16),
            vm((3, ROWS, TILE), BF16),
            vm((3, 3 * R, ROWS), BF16),
            vm((3, 3 * R, ROWS), BF16),
            vm((3, 2, 3, 4, 2, 4, 8, R), F32),
            vm((3, 3, 2, 4, 4, 8, R), F32),
            vm((3, 3, 2, 4, 8, R), F32),
            vm((3, 3, 2, 2, 4, 8, R), F32),
            vm((2, 2, 3, 4, 8, R), F32),
            vm((3, 3, 2, 2, 8, R), F32),
            vm((2, 3, 4, 8, R), F32),
            vm((2, 2, 3, 8, R), F32),
            vm((3, 2, 3, 4, 2, 4, 8, R), F32),
            vm((8, 6, 16, R), F32),
            vm((7, 6, 16, R), F32),
            vm((8, 6, 16, R), F32),
            vm((2, 32, R), F32),
            vm((2, 32, R), F32),
            vm((2, 32, R), F32),
            vm((2, 16, R), F32),
            vm((3, 2, 16, R), F32),
            vm((2, 16, R), F32),
            vm((2, 16, R), F32),
            vm((2, 16, R), F32),
            vm((3, TILE, 3 * R), BF16),
            vm((3, TILE, 3 * R), BF16),
            vm((3, 2 * R, 3 * R), BF16),
            vm((3, R, 3 * R), BF16),
            vm((3, R, 6 * R), BF16),
            vm((3, R, 6 * R), BF16),
            vm((3, R, 6 * R), BF16),
            vm((2, 2, 3, 4, 8, R), F32),
            vm((4, 2, 2, 3, 8, R), F32),
            vm((3, 2, 2, 3, 8, R), F32),
            vm((2, 2, 3, 8, R), F32),
            vm((4, 2, 3, 8, R), F32),
            pltpu.SemaphoreType.DMA((17,)),
            pltpu.SemaphoreType.DMA((NSEM,)),
            pltpu.SemaphoreType.DMA((NSEM,)),
        ],
        compiler_params=pltpu.CompilerParams(
            collective_id=0, has_side_effects=True, vmem_limit_bytes=48 * 1024 * 1024
        ),
        cost_estimate=pl.CostEstimate(flops=14_000_000_000, bytes_accessed=26_000_000, transcendentals=0),
    )(rhs, leaf, e1, p1, c1, e2, p2, c2, e3, p3, c3)


def expand_kernel(y, ehi, elo, corr, out, chi, clo, last, sem):
    done = NR - TILE
    copies = []

    def put(src, dst):
        copy = pltpu.make_async_copy(src, dst, sem.at[len(copies)])
        copy.start()
        copies.append(copy)

    put(y.at[:, :, pl.ds(0, done)], out.at[:, :, pl.ds(0, done)])
    for l in range(3):
        lanes = slice(l * R, (l + 1) * R)
        re, im = corr[l, 0], corr[l, 1]
        for v, value in enumerate((re, im, re + im)):
            chi[v, :, lanes], clo[v, :, lanes] = halves(value)
    cols = pl.ds(done, TILE)
    for q in range(2):
        rows = pl.ds(q * 512, 512)
        re, im = combine([dot_nt(ehi[v, rows, :], elo[v, rows, :], chi[v], clo[v]) for v in range(3)])
        last[0, rows, :] = y[0, rows, cols] - re
        last[1, rows, :] = y[1, rows, cols] - im
        put(last.at[:, rows, :], out.at[:, rows, cols])
    for copy in copies:
        copy.wait()


def expand_call(y, ehi, elo, corr):
    vm = pltpu.VMEM
    return pl.pallas_call(
        expand_kernel,
        out_shape=jax.ShapeDtypeStruct((2, ROWS, NR), F32),
        in_specs=[pl.BlockSpec(memory_space=vm)] * 4,
        out_specs=pl.BlockSpec(memory_space=pltpu.HBM),
        scratch_shapes=[
            vm((3, TILE, 3 * R), BF16),
            vm((3, TILE, 3 * R), BF16),
            vm((2, ROWS, TILE), F32),
            pltpu.SemaphoreType.DMA((3,)),
        ],
        compiler_params=pltpu.CompilerParams(vmem_limit_bytes=20 * 1024 * 1024),
        cost_estimate=pl.CostEstimate(flops=1_800_000_000, bytes_accessed=6_300_000, transcendentals=0),
    )(y, ehi, elo, corr)


def body(rhs, leaf, e1, p1, c1, e2, p2, c2, e3, p3, c3):
    return expand_call(*main_call(rhs, leaf, e1, p1, c1, e2, p2, c2, e3, p3, c3))


def solution(mesh):
    split = P(None, ("wide", "narrow"), None)
    placed = (split, split, split, split, P(None, "wide", None), split, split, P(), split, split, P())
    return jax.shard_map(body, mesh=mesh, in_specs=placed, out_specs=split, check_vma=False)
```

```python
import functools

import jax
import jax.numpy as jnp
from jax import lax
from jax.experimental import pallas as pl
from jax.experimental.pallas import tpu as pltpu
from jax.sharding import PartitionSpec as P

MESH = pl.DeviceIdType.MESH
F32 = jnp.float32
BF16 = jnp.bfloat16
LEAF = 512
R = 128
NR = 768
ROWS = 1024
TILE = 256
NSEM = 120
NT = (((1,), (1,)), ((), ()))


def halves(x):
    hi = x.astype(BF16)
    return hi, (x - hi.astype(F32)).astype(BF16)


def dot_nn(a_hi, a_lo, b_hi, b_lo):
    a = jnp.concatenate([a_hi, a_lo, a_hi], axis=1)
    b = jnp.concatenate([b_hi, b_hi, b_lo], axis=0)
    return jnp.dot(a, b, preferred_element_type=F32)


def dot_nt(a_hi, a_lo, b_hi, b_lo):
    a = jnp.concatenate([a_hi, a_lo, a_hi], axis=1)
    b = jnp.concatenate([b_hi, b_hi, b_lo], axis=1)
    return lax.dot_general(a, b, NT, preferred_element_type=F32)


def combine(t):
    return t[0] - t[1], t[2] - t[0] - t[1]


def small_product(re, im, cat_ref):
    t = []
    for v, x in enumerate((re, im, re + im)):
        hi, lo = halves(x)
        t.append(
            lax.dot_general(
                jnp.concatenate([hi, lo, hi], axis=1),
                cat_ref[v],
                NT,
                preferred_element_type=F32,
            )
        )
    return combine(t)


def store_cat(cat_ref, re, im):
    for v, x in enumerate((re, im, re + im)):
        hi, lo = halves(x)
        cat_ref[v] = jnp.concatenate([hi, hi, lo], axis=1)


def wide_product(re, im, ref):
    c_re, c_im = ref[0], ref[1]
    t = []
    for left, right in ((re, c_re), (im, c_im), (re + im, c_re + c_im)):
        a_hi, a_lo = halves(left)
        b_hi, b_lo = halves(right)
        t.append(dot_nn(a_hi, a_lo, b_hi, b_lo))
    return combine(t)


def main_kernel(
    rhs, leaf, e1, p1, c1, e2, p2, c2, e3, p3, c3,
    rhs_v, ehi, elo, corr_out,
    leaf_v, e_v, p_v, c1_v, c2_v, c3_v,
    lhi, llo, yhi, ylo, pthi, ptlo,
    zt, pair_buf, rs_buf, rzz, zs, ryy, s_buf, p_buf, corr,
    g_loc, g_rs, g_full, h_mine, f_send, f_recv, z_send, z_recv, m_mine, x_send, x_recv,
    chi, clo, hcat, mcat, c1cat, c2cat, c3cat, stk1, tz, rz, stk2, v3,
    in_sem, send_sem, recv_sem,
):
    n = lax.axis_index("narrow")
    w = lax.axis_index("wide")
    y, c = n // 2, lax.rem(n, 2)
    x, z = w // 4, lax.rem(w, 4)
    b, xb = lax.rem(z, 2), lax.rem(x, 2)

    def dev(nn, ww):
        return {"narrow": nn, "wide": ww}

    partner = dev(n + 1 - 2 * c, w)
    sibling = dev(n, w + 1 - 2 * b)
    x_mate = dev(n, w + 4 - 8 * xb)

    def y_at(d):
        return lax.rem(y + d, 4)

    def z_at(d):
        return lax.rem(z + d, 4)

    def y_dev(d):
        return dev(2 * y_at(d) + c, w)

    def z_dev(d):
        return dev(n, x * 4 + z_at(d))

    def x_dev(d):
        return dev(n, lax.rem(x + d, 4) * 4 + z)

    flights = {}
    count = [0]

    def send(key, src, dst, device):
        idx = count[0]
        count[0] += 1
        copy = pltpu.make_async_remote_copy(
            src_ref=src, dst_ref=dst, send_sem=send_sem.at[idx], recv_sem=recv_sem.at[idx],
            device_id=device, device_id_type=MESH,
        )
        copy.start()
        flights[key] = copy

    def arrived(*key):
        flights[key].wait_recv()

    barrier = pltpu.get_barrier_semaphore()
    peers = [dev(lax.rem(n + d, 8), w) for d in range(1, 8)]
    peers += [z_dev(d) for d in range(1, 4)] + [x_dev(d) for d in range(1, 4)]
    for peer in peers:
        pl.semaphore_signal(barrier, inc=1, device_id=peer, device_id_type=MESH)

    pending = {}

    def fetch(name, src, dst):
        copy = pltpu.make_async_copy(src, dst, in_sem.at[len(pending)])
        copy.start()
        pending[name] = copy

    def tile(j):
        return pl.ds(j * TILE, TILE)


    fetch("p2", p2, p_v.at[1])
    fetch("p3", p3, p_v.at[2])
    fetch("e1", e1, e_v.at[0])
    fetch("e2", e2, e_v.at[1])
    for name in ("p2", "p3"):
        pending[name].wait()
    fetch("p1", p1, p_v.at[0])
    fetch("leaf", leaf, leaf_v)

    def prepare_projection(l, carry):
        at = pl.ds(pl.multiple_of(l * R, R), R)
        re, im = p_v[l, 0].T, p_v[l, 1].T
        for v, value in enumerate((re, -im, re - im)):
            pthi[v, at, :], ptlo[v, at, :] = halves(value)
        return carry

    lax.fori_loop(1, 3, prepare_projection, 0)

    pending["e1"].wait()
    pending["e2"].wait()
    fetch("rhs0", rhs.at[:, :, tile(0)], rhs_v.at[:, :, tile(0)])
    fetch("c1", c1, c1_v)
    fetch("c2", c2.at[:, pl.ds(pl.multiple_of(x * R, R), R), :], c2_v)
    fetch("rhs1", rhs.at[:, :, tile(1)], rhs_v.at[:, :, tile(1)])
    re, im = [jnp.concatenate([e_v[0, part], e_v[1, part]], axis=1) for part in range(2)]
    lines = pl.ds(R, 2 * R)
    t = []
    for v, value in enumerate((re, im, re + im)):
        hi, lo = halves(value)
        t.append(dot_nn(pthi[v, lines, :], ptlo[v, lines, :], hi, lo))
    for part, value in enumerate(combine(t)):
        g_loc[:, part] = value[:R, :R].reshape(8, 16, R)
        g_loc[:, 2 + part] = value[R:, :R].reshape(8, 16, R)
        g_loc[:, 4 + part] = value[R:, R:].reshape(8, 16, R)
    pl.semaphore_wait(barrier, len(peers))
    for d in range(1, 8):
        to = lax.rem(n + d, 8)
        send(("g", d), g_loc.at[to], g_rs.at[d - 1], dev(to, w))

    def sides(value, flag):
        left, right = value[:, :R], value[:, R:]
        return jnp.where(flag == 0, left, right), jnp.where(flag == 0, right, left)

    def factor_one():
        for d in range(1, 8):
            arrived("g", d)
        total = g_loc[n]
        for d in range(7):
            total = total + g_rs[d]
        for part in range(2):
            z_send[part] = total[4 + part]
        for d in (2, 1, 3):
            send(("gz", d), z_send, z_recv.at[d - 1], z_dev(d))
        pending["c1"].wait()
        both = wide_product(
            jnp.concatenate([total[0], total[2]], axis=0), jnp.concatenate([total[1], total[3]], axis=0), c1_v
        )
        for part in range(2):
            h_mine[part], f_send[part] = sides(both[part], b)
        send(("f",), f_send, f_recv, sibling)

    def factor_two():
        for d in (2, 1, 3):
            arrived("gz", d)
        total = [z_send[part] + z_recv[0, part] + z_recv[1, part] + z_recv[2, part] for part in range(2)]
        pending["c2"].wait()
        both = wide_product(total[0], total[1], c2_v)
        for part in range(2):
            m_mine[part], x_send[part] = sides(both[part], xb)
        send(("m",), x_send, x_recv, x_mate)

    def factor_three():
        arrived("f")
        arrived("m")
        for part in range(2):
            h = h_mine[part] + f_recv[part]
            g_full[n, part] = h[:16]
            g_full[n, 2 + part] = h[16:]
            g_full[n, 4 + part] = m_mine[part] + x_recv[part]
        for d in range(1, 8):
            send(("ag", d), g_full.at[n], g_full.at[n], dev(lax.rem(n + d, 8), w))

    def factor_four():
        for d in range(1, 8):
            arrived("ag", d)
        h = [jnp.concatenate([g_full[:, part].reshape(R, R), g_full[:, 2 + part].reshape(R, R)], axis=0) for part in range(2)]
        store_cat(hcat, h[0], h[1])
        store_cat(mcat, g_full[:, 4].reshape(R, R), g_full[:, 5].reshape(R, R))

    pending["p1"].wait()
    prepare_projection(0, 0)
    fetch("rhs2", rhs.at[:, :, tile(2)], rhs_v.at[:, :, tile(2)])
    fetch("c3", c3.at[:, pl.ds(pl.multiple_of((x // 2) * R, R), R), :], c3_v)
    fetch("e3", e3, e_v.at[2])
    pending["leaf"].wait()

    def split_leaf(q, carry):
        at = pl.ds(pl.multiple_of(q * 128, 128), 128)
        re, im = leaf_v[0, at, :], leaf_v[1, at, :]
        for v, value in enumerate((re, im, re + im)):
            lhi[v, at, :], llo[v, at, :] = halves(value)
        return carry

    lax.fori_loop(0, 8, split_leaf, 0)
    def solve(j, first, last):
        def one(l, carry):
            rows = pl.ds(pl.multiple_of(l * LEAF, LEAF), LEAF)
            cols = tile(j)
            b_re, b_im = rhs_v[0, rows, cols], rhs_v[1, rows, cols]
            t = []
            for v, value in enumerate((b_re, b_im, b_re + b_im)):
                hi, lo = halves(value)
                t.append(dot_nn(lhi[v, rows, :], llo[v, rows, :], hi, lo))
            re, im = combine(t)
            rhs_v[0, rows, cols] = re
            rhs_v[1, rows, cols] = im
            for v, value in enumerate((re, im, re + im)):
                yhi[v, rows, :], ylo[v, rows, :] = halves(value)
            return carry

        lax.fori_loop(first, last, one, 0)

    def project(j):
        t = [dot_nn(pthi[v], ptlo[v], yhi[v], ylo[v]) for v in range(3)]
        for part, value in enumerate(combine(t)):
            for l in range(3):
                zt[l, part, j] = value[l * R : (l + 1) * R, :].T.reshape(4, 2, 4, 8, R)
        send(("a", j), zt.at[:, :, j, :, 1 - c], pair_buf.at[j], partner)

    def sum_pair(j):
        arrived("a", j)
        zt[:, :, j, :, c] = zt[:, :, j, :, c] + pair_buf[j]
        for d in (2, 1, 3):
            send(("b", j, d), zt.at[0, :, j, y_at(d), c], rs_buf.at[j, d - 1], y_dev(d))
            send(("zz", j, d), zt.at[pl.ds(1, 2), :, j, :, c, z_at(d)], rzz.at[j, d - 1], z_dev(d))

    def sum_z(j):
        for d in (1, 3, 2):
            arrived("zz", j, d)
        zs[:, :, j] = zt[1:3, :, j, :, c, z] + rzz[j, 0] + rzz[j, 1] + rzz[j, 2]
        for d in (2, 1, 3):
            send(("yy", j, d), zs.at[:, :, j, y_at(d)], ryy.at[j, d - 1], y_dev(d))

    def stage_one(g, j0, nj):
        js = pl.ds(j0, nj)
        for j in range(j0, j0 + nj):
            for d in (1, 3, 2):
                arrived("b", j, d)
            s_buf[:, j] = zt[0, :, j, y, c] + rs_buf[j, 0] + rs_buf[j, 1] + rs_buf[j, 2]
        stk1[b, :, js] = s_buf[:, js]
        send(("sib", g), stk1.at[b, :, js], stk1.at[b, :, js], sibling)
        q = small_product(s_buf[0, js].reshape(nj * 32, R), s_buf[1, js].reshape(nj * 32, R), hcat)
        for part in range(2):
            for k in range(2):
                cut = q[part][:, k * R : (k + 1) * R].reshape(nj, 4, 8, R)
                for q4 in range(4):
                    tz[q4, k, part, js] = cut[:, q4]
        for d in (2, 1, 3):
            send(("rz", g, d), tz.at[z_at(d), :, :, js], rz.at[d - 1, :, :, js], z_dev(d))

    def stage_two(g, j0, nj):
        js = pl.ds(j0, nj)
        arrived("sib", g)
        pairs = [
            jnp.concatenate([stk1[p, part, js].reshape(nj * 32, R) for p in range(2)], axis=1) for part in range(2)
        ]
        k1 = small_product(pairs[0], pairs[1], c1cat)
        for part in range(2):
            corr[0, part, js, y, c] = k1[part].reshape(nj, 4, 8, R)
        block = corr.at[0, :, js, y, c]
        send(("p", g, 0), block, block, partner)
        for d in (2, 1, 3):
            send(("s", g, 0, d), block, block, y_dev(d))

    def stage_two_coarse(g, j0, nj):
        js = pl.ds(j0, nj)
        for d in (1, 3, 2):
            arrived("rz", g, d)
        for j in range(j0, j0 + nj):
            for d in (1, 3, 2):
                arrived("yy", j, d)
            total = zs[:, :, j, y] + ryy[j, 0] + ryy[j, 1] + ryy[j, 2]
            p_buf[:, :, j] = total - tz[z, :, :, j] - rz[0, :, :, j] - rz[1, :, :, j] - rz[2, :, :, j]
        stk2[xb, :, js] = p_buf[0, :, js]
        send(("xm", g), stk2.at[xb, :, js], stk2.at[xb, :, js], x_mate)
        m = small_product(p_buf[0, 0, js].reshape(nj * 8, R), p_buf[0, 1, js].reshape(nj * 8, R), mcat)
        for part in range(2):
            v3[x, part, js] = p_buf[1, part, js] - m[part].reshape(nj, 8, R)
        for d in (2, 1, 3):
            send(("v", g, d), v3.at[x, :, js], v3.at[x, :, js], x_dev(d))

    def stage_three(g, j0, nj):
        js = pl.ds(j0, nj)
        arrived("xm", g)
        pairs = [jnp.concatenate([stk2[p, part, js].reshape(nj * 8, R) for p in range(2)], axis=1) for part in range(2)]
        k2 = small_product(pairs[0], pairs[1], c2cat)
        for part in range(2):
            corr[1, part, js, y, c, z] = k2[part].reshape(nj, 8, R)
        piece = corr.at[1, :, js, y, c, z]
        for d in (2, 1, 3):
            send(("u", g, 1, d), piece, piece, z_dev(d))
        for d in (1, 3, 2):
            arrived("v", g, d)
        pairs = [
            jnp.concatenate(
                [(v3[p, part, js] + v3[p + 1, part, js]).reshape(nj * 8, R) for p in (0, 2)], axis=1
            )
            for part in range(2)
        ]
        k3 = small_product(pairs[0], pairs[1], c3cat)
        for part in range(2):
            corr[2, part, js, y, c, z] = k3[part].reshape(nj, 8, R)
        piece = corr.at[2, :, js, y, c, z]
        for d in (2, 1, 3):
            send(("u", g, 2, d), piece, piece, y_dev(d))

    def forward_y(g, l, j0, nj):
        js = pl.ds(j0, nj)
        for d in (1, 3, 2):
            arrived("s", g, l, d)
            block = corr.at[l, :, js, y_at(4 - d), c]
            send(("f", g, l, d), block, block, partner)

    def stage_four(g, j0, nj):
        js = pl.ds(j0, nj)
        for l, block, to in (
            (1, corr.at[1, :, js, y, c], y_dev),
            (2, corr.at[2, :, js, :, c, z], z_dev),
        ):
            for d in (1, 3, 2):
                arrived("u", g, l, d)
            for d in (2, 1, 3):
                send(("s", g, l, d), block, block, to(d))
            send(("p", g, l), block, block, partner)

    def stage_five(g, j0, nj):
        js = pl.ds(j0, nj)
        forward_y(g, 1, j0, nj)
        for d in (1, 3, 2):
            arrived("s", g, 2, d)
            block = corr.at[2, :, js, :, c, z_at(4 - d)]
            send(("f", g, 2, d), block, block, partner)

    def stage_six(g, j0, nj):
        for l in range(3):
            arrived("p", g, l)
            for d in (1, 3, 2):
                arrived("f", g, l, d)
    def prepare_expansion():
        pending["e3"].wait()

        def one(q, carry):
            at = pl.ds(pl.multiple_of(q * 256, 256), 256)
            for l in range(3):
                re, im = e_v[l, 0, at, :], e_v[l, 1, at, :]
                for v, value in enumerate((re, im, re + im)):
                    ehi[v, at, l * R : (l + 1) * R], elo[v, at, l * R : (l + 1) * R] = halves(value)
            return carry

        lax.fori_loop(0, 4, one, 0)

    def expand(j, start, stop):
        cols = tile(j)
        if start == 0:
            for l in range(3):
                lanes = slice(l * R, (l + 1) * R)
                re, im = corr[l, 0, j].reshape(TILE, R), corr[l, 1, j].reshape(TILE, R)
                for v, value in enumerate((re, im, re + im)):
                    chi[v, :, lanes], clo[v, :, lanes] = halves(value)

        def one(q, carry):
            rows = pl.ds(pl.multiple_of(q * 512, 512), 512)
            re, im = combine([dot_nt(ehi[v, rows, :], elo[v, rows, :], chi[v], clo[v]) for v in range(3)])
            rhs_v[0, rows, cols] = rhs_v[0, rows, cols] - re
            rhs_v[1, rows, cols] = rhs_v[1, rows, cols] - im
            return carry

        lax.fori_loop(start, stop, one, 0)

    first, last = (0, 0, 2), (1, 2, 1)
    pending["rhs0"].wait()
    solve(0, 0, 2)
    project(0)
    factor_one()
    pending["rhs1"].wait()
    solve(1, 0, 1)
    sum_pair(0)
    solve(1, 1, 2)
    factor_two()
    project(1)
    sum_z(0)
    pending["rhs2"].wait()
    solve(2, 0, 1)
    sum_pair(1)
    factor_three()
    solve(2, 1, 2)
    sum_z(1)
    project(2)
    factor_four()
    stage_one(*first)
    sum_pair(2)
    pending["c3"].wait()
    store_cat(c1cat, c1_v[0], c1_v[1])
    store_cat(c2cat, c2_v[0], c2_v[1])
    store_cat(c3cat, c3_v[0], c3_v[1])
    prepare_expansion()
    stage_two(*first)
    stage_two_coarse(*first)
    stage_one(*last)
    sum_z(2)
    stage_three(*first)
    stage_two_coarse(*last)
    stage_two(*last)
    stage_four(*first)
    forward_y(*first[:1], 0, *first[1:])
    stage_three(*last)
    stage_five(*first)
    stage_four(*last)
    forward_y(*last[:1], 0, *last[1:])
    stage_six(*first)
    expand(0, 0, 2)
    expand(1, 0, 1)
    stage_five(*last)
    expand(1, 1, 2)
    stage_six(*last)
    for l in range(3):
        for part in range(2):
            corr_out[l, part] = corr[l, part, 2].reshape(TILE, R)

    for copy in flights.values():
        copy.wait_send()


def main_call(rhs, leaf, e1, p1, c1, e2, p2, c2, e3, p3, c3):
    any_spec = pl.BlockSpec(memory_space=pltpu.HBM)
    vm = pltpu.VMEM
    return pl.pallas_call(
        main_kernel,
        out_shape=(
            vm((2, ROWS, NR), F32),
            vm((3, ROWS, 3 * R), BF16),
            vm((3, ROWS, 3 * R), BF16),
            vm((3, 2, TILE, R), F32),
        ),
        in_specs=[any_spec] * 11,
        out_specs=(pl.BlockSpec(memory_space=vm),) * 4,
        scratch_shapes=[
            vm((2, ROWS, LEAF), F32),
            vm((3, 2, ROWS, R), F32),
            vm((3, 2, ROWS, R), F32),
            vm((2, R, 2 * R), F32),
            vm((2, R, 2 * R), F32),
            vm((2, R, 2 * R), F32),
            vm((3, ROWS, LEAF), BF16),
            vm((3, ROWS, LEAF), BF16),
            vm((3, ROWS, TILE), BF16),
            vm((3, ROWS, TILE), BF16),
            vm((3, 3 * R, ROWS), BF16),
            vm((3, 3 * R, ROWS), BF16),
            vm((3, 2, 3, 4, 2, 4, 8, R), F32),
            vm((3, 3, 2, 4, 4, 8, R), F32),
            vm((3, 3, 2, 4, 8, R), F32),
            vm((3, 3, 2, 2, 4, 8, R), F32),
            vm((2, 2, 3, 4, 8, R), F32),
            vm((3, 3, 2, 2, 8, R), F32),
            vm((2, 3, 4, 8, R), F32),
            vm((2, 2, 3, 8, R), F32),
            vm((3, 2, 3, 4, 2, 4, 8, R), F32),
            vm((8, 6, 16, R), F32),
            vm((7, 6, 16, R), F32),
            vm((8, 6, 16, R), F32),
            vm((2, 32, R), F32),
            vm((2, 32, R), F32),
            vm((2, 32, R), F32),
            vm((2, 16, R), F32),
            vm((3, 2, 16, R), F32),
            vm((2, 16, R), F32),
            vm((2, 16, R), F32),
            vm((2, 16, R), F32),
            vm((3, TILE, 3 * R), BF16),
            vm((3, TILE, 3 * R), BF16),
            vm((3, 2 * R, 3 * R), BF16),
            vm((3, R, 3 * R), BF16),
            vm((3, R, 6 * R), BF16),
            vm((3, R, 6 * R), BF16),
            vm((3, R, 6 * R), BF16),
            vm((2, 2, 3, 4, 8, R), F32),
            vm((4, 2, 2, 3, 8, R), F32),
            vm((3, 2, 2, 3, 8, R), F32),
            vm((2, 2, 3, 8, R), F32),
            vm((4, 2, 3, 8, R), F32),
            pltpu.SemaphoreType.DMA((17,)),
            pltpu.SemaphoreType.DMA((NSEM,)),
            pltpu.SemaphoreType.DMA((NSEM,)),
        ],
        compiler_params=pltpu.CompilerParams(
            collective_id=0, has_side_effects=True, vmem_limit_bytes=48 * 1024 * 1024
        ),
        cost_estimate=pl.CostEstimate(flops=14_000_000_000, bytes_accessed=26_000_000, transcendentals=0),
    )(rhs, leaf, e1, p1, c1, e2, p2, c2, e3, p3, c3)


def expand_kernel(y, ehi, elo, corr, out, chi, clo, last, sem):
    done = NR - TILE
    copies = []

    def put(src, dst):
        copy = pltpu.make_async_copy(src, dst, sem.at[len(copies)])
        copy.start()
        copies.append(copy)

    put(y.at[:, :, pl.ds(0, done)], out.at[:, :, pl.ds(0, done)])
    for l in range(3):
        lanes = slice(l * R, (l + 1) * R)
        re, im = corr[l, 0], corr[l, 1]
        for v, value in enumerate((re, im, re + im)):
            chi[v, :, lanes], clo[v, :, lanes] = halves(value)
    cols = pl.ds(done, TILE)
    for q in range(2):
        rows = pl.ds(q * 512, 512)
        re, im = combine([dot_nt(ehi[v, rows, :], elo[v, rows, :], chi[v], clo[v]) for v in range(3)])
        last[0, rows, :] = y[0, rows, cols] - re
        last[1, rows, :] = y[1, rows, cols] - im
        put(last.at[:, rows, :], out.at[:, rows, cols])
    for copy in copies:
        copy.wait()


def expand_call(y, ehi, elo, corr):
    vm = pltpu.VMEM
    return pl.pallas_call(
        expand_kernel,
        out_shape=jax.ShapeDtypeStruct((2, ROWS, NR), F32),
        in_specs=[pl.BlockSpec(memory_space=vm)] * 4,
        out_specs=pl.BlockSpec(memory_space=pltpu.HBM),
        scratch_shapes=[
            vm((3, TILE, 3 * R), BF16),
            vm((3, TILE, 3 * R), BF16),
            vm((2, ROWS, TILE), F32),
            pltpu.SemaphoreType.DMA((3,)),
        ],
        compiler_params=pltpu.CompilerParams(vmem_limit_bytes=20 * 1024 * 1024),
        cost_estimate=pl.CostEstimate(flops=1_800_000_000, bytes_accessed=6_300_000, transcendentals=0),
    )(y, ehi, elo, corr)


def body(rhs, leaf, e1, p1, c1, e2, p2, c2, e3, p3, c3):
    return expand_call(*main_call(rhs, leaf, e1, p1, c1, e2, p2, c2, e3, p3, c3))


def solution(mesh):
    split = P(None, ("wide", "narrow"), None)
    placed = (split, split, split, split, P(None, "wide", None), split, split, P(), split, split, P())
    return jax.shard_map(body, mesh=mesh, in_specs=placed, out_specs=split, check_vma=False)
```

```python
import functools

import jax
import jax.numpy as jnp
from jax import lax
from jax.experimental import pallas as pl
from jax.experimental.pallas import tpu as pltpu
from jax.sharding import PartitionSpec as P

MESH = pl.DeviceIdType.MESH
F32 = jnp.float32
BF16 = jnp.bfloat16
LEAF = 512
R = 128
NR = 768
ROWS = 1024
TILE = 256
NSEM = 120
NT = (((1,), (1,)), ((), ()))


def halves(x):
    hi = x.astype(BF16)
    return hi, (x - hi.astype(F32)).astype(BF16)


def dot_nn(a_hi, a_lo, b_hi, b_lo):
    a = jnp.concatenate([a_hi, a_lo, a_hi], axis=1)
    b = jnp.concatenate([b_hi, b_hi, b_lo], axis=0)
    return jnp.dot(a, b, preferred_element_type=F32)


def dot_nt(a_hi, a_lo, b_hi, b_lo):
    a = jnp.concatenate([a_hi, a_lo, a_hi], axis=1)
    b = jnp.concatenate([b_hi, b_hi, b_lo], axis=1)
    return lax.dot_general(a, b, NT, preferred_element_type=F32)


def combine(t):
    return t[0] - t[1], t[2] - t[0] - t[1]


def small_product(re, im, cat_ref):
    t = []
    for v, x in enumerate((re, im, re + im)):
        hi, lo = halves(x)
        t.append(
            lax.dot_general(
                jnp.concatenate([hi, lo, hi], axis=1),
                cat_ref[v],
                NT,
                preferred_element_type=F32,
            )
        )
    return combine(t)


def store_cat(cat_ref, re, im):
    for v, x in enumerate((re, im, re + im)):
        hi, lo = halves(x)
        cat_ref[v] = jnp.concatenate([hi, hi, lo], axis=1)


def wide_product(re, im, ref):
    c_re, c_im = ref[0], ref[1]
    t = []
    for left, right in ((re, c_re), (im, c_im), (re + im, c_re + c_im)):
        a_hi, a_lo = halves(left)
        b_hi, b_lo = halves(right)
        t.append(dot_nn(a_hi, a_lo, b_hi, b_lo))
    return combine(t)


def main_kernel(
    rhs, leaf, e1, p1, c1, e2, p2, c2, e3, p3, c3,
    rhs_v, ehi, elo, corr_out,
    leaf_v, e_v, p_v, c1_v, c2_v, c3_v,
    lhi, llo, yhi, ylo, pthi, ptlo,
    zt, pair_buf, rs_buf, rzz, zs, ryy, s_buf, p_buf, corr,
    g_loc, g_rs, g_full, h_mine, f_send, f_recv, z_send, z_recv, m_mine, x_send, x_recv,
    chi, clo, hcat, mcat, c1cat, c2cat, c3cat, stk1, tz, rz, stk2, v3,
    in_sem, send_sem, recv_sem,
):
    n = lax.axis_index("narrow")
    w = lax.axis_index("wide")
    y, c = n // 2, lax.rem(n, 2)
    x, z = w // 4, lax.rem(w, 4)
    b, xb = lax.rem(z, 2), lax.rem(x, 2)

    def dev(nn, ww):
        return {"narrow": nn, "wide": ww}

    partner = dev(n + 1 - 2 * c, w)
    sibling = dev(n, w + 1 - 2 * b)
    x_mate = dev(n, w + 4 - 8 * xb)

    def y_at(d):
        return lax.rem(y + d, 4)

    def z_at(d):
        return lax.rem(z + d, 4)

    def y_dev(d):
        return dev(2 * y_at(d) + c, w)

    def z_dev(d):
        return dev(n, x * 4 + z_at(d))

    def x_dev(d):
        return dev(n, lax.rem(x + d, 4) * 4 + z)

    flights = {}
    count = [0]

    def send(key, src, dst, device):
        idx = count[0]
        count[0] += 1
        copy = pltpu.make_async_remote_copy(
            src_ref=src, dst_ref=dst, send_sem=send_sem.at[idx], recv_sem=recv_sem.at[idx],
            device_id=device, device_id_type=MESH,
        )
        copy.start()
        flights[key] = copy

    def arrived(*key):
        flights[key].wait_recv()

    barrier = pltpu.get_barrier_semaphore()
    peers = [dev(lax.rem(n + d, 8), w) for d in range(1, 8)]
    peers += [z_dev(d) for d in range(1, 4)] + [x_dev(d) for d in range(1, 4)]
    for peer in peers:
        pl.semaphore_signal(barrier, inc=1, device_id=peer, device_id_type=MESH)

    pending = {}

    def fetch(name, src, dst):
        copy = pltpu.make_async_copy(src, dst, in_sem.at[len(pending)])
        copy.start()
        pending[name] = copy

    def tile(j):
        return pl.ds(j * TILE, TILE)


    fetch("p2", p2, p_v.at[1])
    fetch("p3", p3, p_v.at[2])
    fetch("e1", e1, e_v.at[0])
    fetch("e2", e2, e_v.at[1])
    for name in ("p2", "p3"):
        pending[name].wait()
    fetch("p1", p1, p_v.at[0])
    fetch("leaf", leaf, leaf_v)

    def prepare_projection(l, carry):
        at = pl.ds(pl.multiple_of(l * R, R), R)
        re, im = p_v[l, 0].T, p_v[l, 1].T
        for v, value in enumerate((re, -im, re - im)):
            pthi[v, at, :], ptlo[v, at, :] = halves(value)
        return carry

    lax.fori_loop(1, 3, prepare_projection, 0)

    pending["e1"].wait()
    pending["e2"].wait()
    fetch("rhs0", rhs.at[:, :, tile(0)], rhs_v.at[:, :, tile(0)])
    fetch("c1", c1, c1_v)
    fetch("c2", c2.at[:, pl.ds(pl.multiple_of(x * R, R), R), :], c2_v)
    fetch("rhs1", rhs.at[:, :, tile(1)], rhs_v.at[:, :, tile(1)])
    re, im = [jnp.concatenate([e_v[0, part], e_v[1, part]], axis=1) for part in range(2)]
    lines = pl.ds(R, 2 * R)
    t = []
    for v, value in enumerate((re, im, re + im)):
        hi, lo = halves(value)
        t.append(dot_nn(pthi[v, lines, :], ptlo[v, lines, :], hi, lo))
    for part, value in enumerate(combine(t)):
        g_loc[:, part] = value[:R, :R].reshape(8, 16, R)
        g_loc[:, 2 + part] = value[R:, :R].reshape(8, 16, R)
        g_loc[:, 4 + part] = value[R:, R:].reshape(8, 16, R)
    pl.semaphore_wait(barrier, len(peers))
    for d in range(1, 8):
        to = lax.rem(n + d, 8)
        send(("g", d), g_loc.at[to], g_rs.at[d - 1], dev(to, w))

    def sides(value, flag):
        left, right = value[:, :R], value[:, R:]
        return jnp.where(flag == 0, left, right), jnp.where(flag == 0, right, left)

    def factor_one():
        for d in range(1, 8):
            arrived("g", d)
        total = g_loc[n]
        for d in range(7):
            total = total + g_rs[d]
        for part in range(2):
            z_send[part] = total[4 + part]
        for d in (2, 1, 3):
            send(("gz", d), z_send, z_recv.at[d - 1], z_dev(d))
        pending["c1"].wait()
        both = wide_product(
            jnp.concatenate([total[0], total[2]], axis=0), jnp.concatenate([total[1], total[3]], axis=0), c1_v
        )
        for part in range(2):
            h_mine[part], f_send[part] = sides(both[part], b)
        send(("f",), f_send, f_recv, sibling)

    def factor_two():
        for d in (2, 1, 3):
            arrived("gz", d)
        total = [z_send[part] + z_recv[0, part] + z_recv[1, part] + z_recv[2, part] for part in range(2)]
        pending["c2"].wait()
        both = wide_product(total[0], total[1], c2_v)
        for part in range(2):
            m_mine[part], x_send[part] = sides(both[part], xb)
        send(("m",), x_send, x_recv, x_mate)

    def factor_three():
        arrived("f")
        arrived("m")
        for part in range(2):
            h = h_mine[part] + f_recv[part]
            g_full[n, part] = h[:16]
            g_full[n, 2 + part] = h[16:]
            g_full[n, 4 + part] = m_mine[part] + x_recv[part]
        for d in range(1, 8):
            send(("ag", d), g_full.at[n], g_full.at[n], dev(lax.rem(n + d, 8), w))

    def factor_four():
        for d in range(1, 8):
            arrived("ag", d)
        h = [jnp.concatenate([g_full[:, part].reshape(R, R), g_full[:, 2 + part].reshape(R, R)], axis=0) for part in range(2)]
        store_cat(hcat, h[0], h[1])
        store_cat(mcat, g_full[:, 4].reshape(R, R), g_full[:, 5].reshape(R, R))

    pending["p1"].wait()
    prepare_projection(0, 0)
    fetch("rhs2", rhs.at[:, :, tile(2)], rhs_v.at[:, :, tile(2)])
    fetch("c3", c3.at[:, pl.ds(pl.multiple_of((x // 2) * R, R), R), :], c3_v)
    fetch("e3", e3, e_v.at[2])
    pending["leaf"].wait()

    def split_leaf(q, carry):
        at = pl.ds(pl.multiple_of(q * 128, 128), 128)
        re, im = leaf_v[0, at, :], leaf_v[1, at, :]
        for v, value in enumerate((re, im, re + im)):
            lhi[v, at, :], llo[v, at, :] = halves(value)
        return carry

    lax.fori_loop(0, 8, split_leaf, 0)
    def solve(j, first, last):
        def one(l, carry):
            rows = pl.ds(pl.multiple_of(l * LEAF, LEAF), LEAF)
            cols = tile(j)
            b_re, b_im = rhs_v[0, rows, cols], rhs_v[1, rows, cols]
            t = []
            for v, value in enumerate((b_re, b_im, b_re + b_im)):
                hi, lo = halves(value)
                t.append(dot_nn(lhi[v, rows, :], llo[v, rows, :], hi, lo))
            re, im = combine(t)
            rhs_v[0, rows, cols] = re
            rhs_v[1, rows, cols] = im
            for v, value in enumerate((re, im, re + im)):
                yhi[v, rows, :], ylo[v, rows, :] = halves(value)
            return carry

        lax.fori_loop(first, last, one, 0)

    def project(j):
        t = [dot_nn(pthi[v], ptlo[v], yhi[v], ylo[v]) for v in range(3)]
        for part, value in enumerate(combine(t)):
            for l in range(3):
                zt[l, part, j] = value[l * R : (l + 1) * R, :].T.reshape(4, 2, 4, 8, R)
        send(("a", j), zt.at[:, :, j, :, 1 - c], pair_buf.at[j], partner)

    def sum_pair(j):
        arrived("a", j)
        zt[:, :, j, :, c] = zt[:, :, j, :, c] + pair_buf[j]
        for d in (2, 1, 3):
            send(("b", j, d), zt.at[0, :, j, y_at(d), c], rs_buf.at[j, d - 1], y_dev(d))
            send(("zz", j, d), zt.at[pl.ds(1, 2), :, j, :, c, z_at(d)], rzz.at[j, d - 1], z_dev(d))

    def sum_z(j):
        for d in (1, 3, 2):
            arrived("zz", j, d)
        zs[:, :, j] = zt[1:3, :, j, :, c, z] + rzz[j, 0] + rzz[j, 1] + rzz[j, 2]
        for d in (2, 1, 3):
            send(("yy", j, d), zs.at[:, :, j, y_at(d)], ryy.at[j, d - 1], y_dev(d))

    def stage_one(g, j0, nj):
        js = pl.ds(j0, nj)
        for j in range(j0, j0 + nj):
            for d in (1, 3, 2):
                arrived("b", j, d)
            s_buf[:, j] = zt[0, :, j, y, c] + rs_buf[j, 0] + rs_buf[j, 1] + rs_buf[j, 2]
        stk1[b, :, js] = s_buf[:, js]
        send(("sib", g), stk1.at[b, :, js], stk1.at[b, :, js], sibling)
        q = small_product(s_buf[0, js].reshape(nj * 32, R), s_buf[1, js].reshape(nj * 32, R), hcat)
        for part in range(2):
            for k in range(2):
                cut = q[part][:, k * R : (k + 1) * R].reshape(nj, 4, 8, R)
                for q4 in range(4):
                    tz[q4, k, part, js] = cut[:, q4]
        for d in (2, 1, 3):
            send(("rz", g, d), tz.at[z_at(d), :, :, js], rz.at[d - 1, :, :, js], z_dev(d))

    def stage_two(g, j0, nj):
        js = pl.ds(j0, nj)
        arrived("sib", g)
        pairs = [
            jnp.concatenate([stk1[p, part, js].reshape(nj * 32, R) for p in range(2)], axis=1) for part in range(2)
        ]
        k1 = small_product(pairs[0], pairs[1], c1cat)
        for part in range(2):
            corr[0, part, js, y, c] = k1[part].reshape(nj, 4, 8, R)
        block = corr.at[0, :, js, y, c]
        send(("p", g, 0), block, block, partner)
        for d in (2, 1, 3):
            send(("s", g, 0, d), block, block, y_dev(d))

    def stage_two_coarse(g, j0, nj):
        js = pl.ds(j0, nj)
        for d in (1, 3, 2):
            arrived("rz", g, d)
        for j in range(j0, j0 + nj):
            for d in (1, 3, 2):
                arrived("yy", j, d)
            total = zs[:, :, j, y] + ryy[j, 0] + ryy[j, 1] + ryy[j, 2]
            p_buf[:, :, j] = total - tz[z, :, :, j] - rz[0, :, :, j] - rz[1, :, :, j] - rz[2, :, :, j]
        stk2[xb, :, js] = p_buf[0, :, js]
        send(("xm", g), stk2.at[xb, :, js], stk2.at[xb, :, js], x_mate)
        m = small_product(p_buf[0, 0, js].reshape(nj * 8, R), p_buf[0, 1, js].reshape(nj * 8, R), mcat)
        for part in range(2):
            v3[x, part, js] = p_buf[1, part, js] - m[part].reshape(nj, 8, R)
        for d in (2, 1, 3):
            send(("v", g, d), v3.at[x, :, js], v3.at[x, :, js], x_dev(d))

    def stage_three(g, j0, nj):
        js = pl.ds(j0, nj)
        arrived("xm", g)
        pairs = [jnp.concatenate([stk2[p, part, js].reshape(nj * 8, R) for p in range(2)], axis=1) for part in range(2)]
        k2 = small_product(pairs[0], pairs[1], c2cat)
        for part in range(2):
            corr[1, part, js, y, c, z] = k2[part].reshape(nj, 8, R)
        piece = corr.at[1, :, js, y, c, z]
        for d in (2, 1, 3):
            send(("u", g, 1, d), piece, piece, z_dev(d))
        for d in (1, 3, 2):
            arrived("v", g, d)
        pairs = [
            jnp.concatenate(
                [(v3[p, part, js] + v3[p + 1, part, js]).reshape(nj * 8, R) for p in (0, 2)], axis=1
            )
            for part in range(2)
        ]
        k3 = small_product(pairs[0], pairs[1], c3cat)
        for part in range(2):
            corr[2, part, js, y, c, z] = k3[part].reshape(nj, 8, R)
        piece = corr.at[2, :, js, y, c, z]
        for d in (2, 1, 3):
            send(("u", g, 2, d), piece, piece, y_dev(d))

    def forward_y(g, l, j0, nj):
        js = pl.ds(j0, nj)
        for d in (1, 3, 2):
            arrived("s", g, l, d)
            block = corr.at[l, :, js, y_at(4 - d), c]
            send(("f", g, l, d), block, block, partner)

    def stage_four(g, j0, nj):
        js = pl.ds(j0, nj)
        for l, block, to in (
            (1, corr.at[1, :, js, y, c], y_dev),
            (2, corr.at[2, :, js, :, c, z], z_dev),
        ):
            for d in (1, 3, 2):
                arrived("u", g, l, d)
            for d in (2, 1, 3):
                send(("s", g, l, d), block, block, to(d))
            send(("p", g, l), block, block, partner)

    def stage_five(g, j0, nj):
        js = pl.ds(j0, nj)
        forward_y(g, 1, j0, nj)
        for d in (1, 3, 2):
            arrived("s", g, 2, d)
            block = corr.at[2, :, js, :, c, z_at(4 - d)]
            send(("f", g, 2, d), block, block, partner)

    def stage_six(g, j0, nj):
        for l in range(3):
            arrived("p", g, l)
            for d in (1, 3, 2):
                arrived("f", g, l, d)
    def prepare_expansion():
        pending["e3"].wait()

        def one(q, carry):
            at = pl.ds(pl.multiple_of(q * 256, 256), 256)
            for l in range(3):
                re, im = e_v[l, 0, at, :], e_v[l, 1, at, :]
                for v, value in enumerate((re, im, re + im)):
                    ehi[v, at, l * R : (l + 1) * R], elo[v, at, l * R : (l + 1) * R] = halves(value)
            return carry

        lax.fori_loop(0, 4, one, 0)

    def expand(j, start, stop):
        cols = tile(j)
        if start == 0:
            for l in range(3):
                lanes = slice(l * R, (l + 1) * R)
                re, im = corr[l, 0, j].reshape(TILE, R), corr[l, 1, j].reshape(TILE, R)
                for v, value in enumerate((re, im, re + im)):
                    chi[v, :, lanes], clo[v, :, lanes] = halves(value)

        def one(q, carry):
            rows = pl.ds(pl.multiple_of(q * 512, 512), 512)
            re, im = combine([dot_nt(ehi[v, rows, :], elo[v, rows, :], chi[v], clo[v]) for v in range(3)])
            rhs_v[0, rows, cols] = rhs_v[0, rows, cols] - re
            rhs_v[1, rows, cols] = rhs_v[1, rows, cols] - im
            return carry

        lax.fori_loop(start, stop, one, 0)

    first, last = (0, 0, 2), (1, 2, 1)
    pending["rhs0"].wait()
    solve(0, 0, 2)
    project(0)
    factor_one()
    pending["rhs1"].wait()
    solve(1, 0, 1)
    sum_pair(0)
    solve(1, 1, 2)
    factor_two()
    project(1)
    sum_z(0)
    pending["rhs2"].wait()
    solve(2, 0, 1)
    sum_pair(1)
    factor_three()
    solve(2, 1, 2)
    sum_z(1)
    project(2)
    factor_four()
    stage_one(*first)
    sum_pair(2)
    pending["c3"].wait()
    store_cat(c1cat, c1_v[0], c1_v[1])
    store_cat(c2cat, c2_v[0], c2_v[1])
    store_cat(c3cat, c3_v[0], c3_v[1])
    prepare_expansion()
    stage_two(*first)
    stage_two_coarse(*first)
    stage_one(*last)
    sum_z(2)
    stage_three(*first)
    stage_two_coarse(*last)
    stage_two(*last)
    stage_four(*first)
    forward_y(*first[:1], 0, *first[1:])
    stage_three(*last)
    stage_five(*first)
    stage_four(*last)
    forward_y(*last[:1], 0, *last[1:])
    stage_six(*first)
    expand(0, 0, 2)
    expand(1, 0, 1)
    stage_five(*last)
    expand(1, 1, 2)
    stage_six(*last)
    for l in range(3):
        for part in range(2):
            corr_out[l, part] = corr[l, part, 2].reshape(TILE, R)

    for copy in flights.values():
        copy.wait_send()


def main_call(rhs, leaf, e1, p1, c1, e2, p2, c2, e3, p3, c3):
    any_spec = pl.BlockSpec(memory_space=pltpu.HBM)
    vm = pltpu.VMEM
    return pl.pallas_call(
        main_kernel,
        out_shape=(
            vm((2, ROWS, NR), F32),
            vm((3, ROWS, 3 * R), BF16),
            vm((3, ROWS, 3 * R), BF16),
            vm((3, 2, TILE, R), F32),
        ),
        in_specs=[any_spec] * 11,
        out_specs=(pl.BlockSpec(memory_space=vm),) * 4,
        scratch_shapes=[
            vm((2, ROWS, LEAF), F32),
            vm((3, 2, ROWS, R), F32),
            vm((3, 2, ROWS, R), F32),
            vm((2, R, 2 * R), F32),
            vm((2, R, 2 * R), F32),
            vm((2, R, 2 * R), F32),
            vm((3, ROWS, LEAF), BF16),
            vm((3, ROWS, LEAF), BF16),
            vm((3, ROWS, TILE), BF16),
            vm((3, ROWS, TILE), BF16),
            vm((3, 3 * R, ROWS), BF16),
            vm((3, 3 * R, ROWS), BF16),
            vm((3, 2, 3, 4, 2, 4, 8, R), F32),
            vm((3, 3, 2, 4, 4, 8, R), F32),
            vm((3, 3, 2, 4, 8, R), F32),
            vm((3, 3, 2, 2, 4, 8, R), F32),
            vm((2, 2, 3, 4, 8, R), F32),
            vm((3, 3, 2, 2, 8, R), F32),
            vm((2, 3, 4, 8, R), F32),
            vm((2, 2, 3, 8, R), F32),
            vm((3, 2, 3, 4, 2, 4, 8, R), F32),
            vm((8, 6, 16, R), F32),
            vm((7, 6, 16, R), F32),
            vm((8, 6, 16, R), F32),
            vm((2, 32, R), F32),
            vm((2, 32, R), F32),
            vm((2, 32, R), F32),
            vm((2, 16, R), F32),
            vm((3, 2, 16, R), F32),
            vm((2, 16, R), F32),
            vm((2, 16, R), F32),
            vm((2, 16, R), F32),
            vm((3, TILE, 3 * R), BF16),
            vm((3, TILE, 3 * R), BF16),
            vm((3, 2 * R, 3 * R), BF16),
            vm((3, R, 3 * R), BF16),
            vm((3, R, 6 * R), BF16),
            vm((3, R, 6 * R), BF16),
            vm((3, R, 6 * R), BF16),
            vm((2, 2, 3, 4, 8, R), F32),
            vm((4, 2, 2, 3, 8, R), F32),
            vm((3, 2, 2, 3, 8, R), F32),
            vm((2, 2, 3, 8, R), F32),
            vm((4, 2, 3, 8, R), F32),
            pltpu.SemaphoreType.DMA((17,)),
            pltpu.SemaphoreType.DMA((NSEM,)),
            pltpu.SemaphoreType.DMA((NSEM,)),
        ],
        compiler_params=pltpu.CompilerParams(
            collective_id=0, has_side_effects=True, vmem_limit_bytes=48 * 1024 * 1024
        ),
        cost_estimate=pl.CostEstimate(flops=14_000_000_000, bytes_accessed=26_000_000, transcendentals=0),
    )(rhs, leaf, e1, p1, c1, e2, p2, c2, e3, p3, c3)


def expand_kernel(y, ehi, elo, corr, out, chi, clo, last, sem):
    done = NR - TILE
    copies = []

    def put(src, dst):
        copy = pltpu.make_async_copy(src, dst, sem.at[len(copies)])
        copy.start()
        copies.append(copy)

    put(y.at[:, :, pl.ds(0, done)], out.at[:, :, pl.ds(0, done)])
    for l in range(3):
        lanes = slice(l * R, (l + 1) * R)
        re, im = corr[l, 0], corr[l, 1]
        for v, value in enumerate((re, im, re + im)):
            chi[v, :, lanes], clo[v, :, lanes] = halves(value)
    cols = pl.ds(done, TILE)
    for q in range(4):
        rows = pl.ds(q * 256, 256)
        re, im = combine([dot_nt(ehi[v, rows, :], elo[v, rows, :], chi[v], clo[v]) for v in range(3)])
        last[0, rows, :] = y[0, rows, cols] - re
        last[1, rows, :] = y[1, rows, cols] - im
        put(last.at[:, rows, :], out.at[:, rows, cols])
    for copy in copies:
        copy.wait()


def expand_call(y, ehi, elo, corr):
    vm = pltpu.VMEM
    return pl.pallas_call(
        expand_kernel,
        out_shape=jax.ShapeDtypeStruct((2, ROWS, NR), F32),
        in_specs=[pl.BlockSpec(memory_space=vm)] * 4,
        out_specs=pl.BlockSpec(memory_space=pltpu.HBM),
        scratch_shapes=[
            vm((3, TILE, 3 * R), BF16),
            vm((3, TILE, 3 * R), BF16),
            vm((2, ROWS, TILE), F32),
            pltpu.SemaphoreType.DMA((5,)),
        ],
        compiler_params=pltpu.CompilerParams(vmem_limit_bytes=20 * 1024 * 1024),
        cost_estimate=pl.CostEstimate(flops=1_800_000_000, bytes_accessed=6_300_000, transcendentals=0),
    )(y, ehi, elo, corr)


def body(rhs, leaf, e1, p1, c1, e2, p2, c2, e3, p3, c3):
    return expand_call(*main_call(rhs, leaf, e1, p1, c1, e2, p2, c2, e3, p3, c3))


def solution(mesh):
    split = P(None, ("wide", "narrow"), None)
    placed = (split, split, split, split, P(None, "wide", None), split, split, P(), split, split, P())
    return jax.shard_map(body, mesh=mesh, in_specs=placed, out_specs=split, check_vma=False)
```
